768 devices in a mesh: ctx: 32 (over y, x), dp: 24 (over z, core).
Axes of the slice: x: 4, y: 8, z: 12, core: 2. Of those that a mesh axis runs over, the one named last changes fastest.
Arguments:
- queries: bfloat16 [24, 2, 2048, 512], P('dp', None, 'ctx'), may hold values from -6 to 6
- key_vectors: bfloat16 [24, 2, 2048, 512], P('dp', None, 'ctx'), may hold values from -6 to 6
- value_vectors: bfloat16 [24, 2, 2048, 1024], P('dp', None, 'ctx'), may hold values from -6 to 6
- out_grad: bfloat16 [24, 2, 2048, 1024], P('dp', None, 'ctx'), may hold values from -6 to 6
- forget_logits: bfloat16 [24, 2, 4, 2048], P('dp', None, None, 'ctx'), may hold values from 0 to 16
- input_logits: bfloat16 [24, 2, 4, 2048], P('dp', None, None, 'ctx'), may hold values from -6 to 6
- norm_gain: bfloat16 [1024], replicated, may hold values from 0.099609375 to 1.8984375
Outputs:
- grad_queries: bfloat16 [24, 2, 2048, 512], P('dp', None, 'ctx')
- grad_keys: bfloat16 [24, 2, 2048, 512], P('dp', None, 'ctx')
- grad_values: bfloat16 [24, 2, 2048, 1024], P('dp', None, 'ctx')
- grad_forget: float32 [24, 2, 4, 2048], P('dp', None, None, 'ctx')
- grad_input: float32 [24, 2, 4, 2048], P('dp', None, None, 'ctx')
- grad_gain: float32 [1024], replicated
The draws below stay inside these ranges and needn't reach their ends.
All inputs are finite; a program needn't handle non-finite values.
Results may differ from the reference program's by a relative error of at most 0.04.
Values sent between devices are 32-bit elements; how exact they have to be, the bound alone decides.
A program may use at most 128 MiB of HBM per device.

```python
import jax
import jax.numpy as jnp
from jax import lax

H = 4
DK = 128
DV = 256
CH = 64
B = 24
HALF = 2048
SEQUENCE_LENGTH = 4096
N_CTX = 32


def draw_forget_logits(key, part):
    variety_random_key, random_key_root, block_random_key, token_random_key, spike_random_key, height_random_key = jax.random.split(key, 6)
    complete_shape = (B, 2, H, HALF)
    fast_share = 0.5
    kind_draw = jax.random.uniform(variety_random_key, (B, 1, H, 1))
    base_draw = jax.random.uniform(random_key_root, (B, 1, H, 1))
    slow_rate = jnp.exp(jnp.log(0.03) + base_draw * (jnp.log(0.3) - jnp.log(0.03))) / SEQUENCE_LENGTH
    fast_rate = jnp.exp(jnp.log(1.0 / 50.0) + base_draw * (jnp.log(1.0 / 30.0) - jnp.log(1.0 / 50.0)))
    base_rate = jnp.where(kind_draw < fast_share, fast_rate, slow_rate)
    block_factor = jnp.exp(jax.random.uniform(block_random_key, (B, 2, H, HALF // CH, 1), minval=-0.35, maxval=0.35))
    block_factor = jnp.broadcast_to(block_factor, (B, 2, H, HALF // CH, CH)).reshape(complete_shape)
    token_factor = jnp.exp(jax.random.uniform(token_random_key, complete_shape, minval=-0.35, maxval=0.35))
    rate_all = base_rate * block_factor * token_factor
    constant_level = jnp.log(1.0 / rate_all - 1.0)
    spike_position = jax.random.uniform(spike_random_key, complete_shape) < 2.5 / SEQUENCE_LENGTH
    spike_height = jax.random.uniform(height_random_key, complete_shape, minval=0.0, maxval=1.386)
    return jnp.clip(jnp.where(spike_position, spike_height, constant_level), 0.0, 16.0).astype(jnp.bfloat16)


def steps_of(stream_key, dims, cuts, least, top_value):
    loudness = 1.0
    for position, blocks in cuts:
        draws = jax.random.uniform(jax.random.fold_in(jax.random.fold_in(stream_key, 6), position), (blocks,), jnp.float32, least / len(cuts), top_value / len(cuts))
        loudness = loudness * jnp.repeat(jnp.exp(draws), dims[position] // blocks).reshape((-1,) + (1,) * (len(dims) - 1 - position))
    return loudness


def noise(own_key, dims, scale, limit, pieces=(), dtype=jnp.bfloat16):
    factor_of = steps_of(own_key, dims, pieces, -0.22, 0.18) if pieces else 1.0
    entries = jax.random.normal(own_key, dims, jnp.float32) * scale * factor_of
    return jnp.minimum(jnp.maximum(entries, -limit), limit).astype(dtype)


def setup_inputs(seed: int = 0) -> dict:
    key_list = jax.random.split(jax.random.key(seed), 8)
    return {
        "queries": noise(key_list[0], (B, 2, HALF, H * DK), 1.0, 6.0, ((0, 24), (2, 32))),
        "key_vectors": noise(key_list[1], (B, 2, HALF, H * DK), 1.0, 6.0, ((0, 24), (2, 32))),
        "value_vectors": noise(key_list[2], (B, 2, HALF, H * DV), 1.0, 6.0, ((0, 24), (2, 32))),
        "out_grad": noise(key_list[3], (B, 2, HALF, H * DV), 1.0, 6.0, ((0, 24), (2, 32))),
        "forget_logits": draw_forget_logits(jax.random.fold_in(key_list[7], 71), 0),
        "input_logits": noise(key_list[5], (B, 2, H, HALF), 1.5, 6.0, ((0, 24), (3, 32))),
        "norm_gain": jnp.clip(1.0 + 0.18 * jax.random.normal(key_list[6], (H * DV,), jnp.float32), 0.099609375, 1.8984375).astype(jnp.bfloat16),
    }


def multiply(form, left, right):
    return jnp.einsum(form, left.astype(jnp.float32), right.astype(jnp.float32))

def gate_terms(forget_in, input_in):
    forget_logit = forget_in.astype(jnp.float32)
    cum_log = jnp.cumsum(jax.nn.log_sigmoid(forget_logit), axis=-1)
    fade_total = cum_log[..., -1]
    ingate = jax.nn.sigmoid(input_in.astype(jnp.float32))
    span_len = cum_log.shape[-1]
    row_ids = lax.broadcasted_iota(jnp.int32, (span_len, span_len), 0)
    col_ids = lax.broadcasted_iota(jnp.int32, (span_len, span_len), 1)
    causal = row_ids >= col_ids
    spread = cum_log[..., :, None] - cum_log[..., None, :]
    decay_mat = jnp.where(causal, jnp.exp(jnp.where(causal, spread, 0.0)), 0.0)
    reach_fade = jnp.exp(fade_total[..., None] - cum_log)
    return (forget_logit, ingate, cum_log, fade_total, decay_mat, reach_fade)

def block_write(key_part, value_part, ingate, reach_fade):
    weights = jnp.swapaxes(ingate * reach_fade, -1, -2)[..., None]
    scaled = (value_part.astype(jnp.float32) * weights).astype(jnp.bfloat16)
    return multiply('...shd,...shv->...hdv', key_part, scaled)

def block_read(query_part, key_part, value_part, ingate, cum_log, decay_mat, state_in):
    scores = multiply('...thd,...shd->...hts', query_part, key_part)
    mix_weights = (scores * decay_mat * ingate[..., None, :]).astype(jnp.bfloat16)
    state_b = state_in.astype(jnp.bfloat16)
    early_fade = jnp.swapaxes(jnp.exp(cum_log), -1, -2)[..., None]
    hidden = multiply('...hts,...shv->...thv', mix_weights, value_part) + early_fade * multiply('...thd,...hdv->...thv', query_part, state_b)
    return (scores, mix_weights, state_b, hidden, early_fade)

def norm_back(hidden, out_part, gain_rows, early_fade, query_part):
    square = lax.optimization_barrier(jnp.mean(hidden * hidden, axis=-1, keepdims=True))
    inv_rms = lax.rsqrt(square + 1e-05)
    normed = hidden * inv_rms
    pushed = out_part.astype(jnp.float32) * gain_rows
    center = lax.optimization_barrier(jnp.mean(pushed * normed, axis=-1, keepdims=True))
    grad_hidden = inv_rms * (pushed - normed * center)
    grad_b = grad_hidden.astype(jnp.bfloat16)
    lifted = (grad_hidden * early_fade).astype(jnp.bfloat16)
    back_write = multiply('...thd,...thv->...hdv', query_part, lifted)
    return (grad_hidden, grad_b, normed, back_write)

def block_grads(query_part, key_part, value_part, ingate, reach_fade, decay_mat, early_fade, scores, mix_weights, state_b, hidden, grad_hidden, grad_b, later_state):
    pushed = multiply('...thv,...shv->...hts', grad_b, value_part)
    attend = (pushed * decay_mat * ingate[..., None, :]).astype(jnp.bfloat16)
    later_b = later_state.astype(jnp.bfloat16)
    weights = jnp.swapaxes(ingate * reach_fade, -1, -2)[..., None]
    carried = multiply('...shv,...hdv->...shd', value_part, later_b)
    grad_q = multiply('...hts,...shd->...thd', attend, key_part) + early_fade * multiply('...thv,...hdv->...thd', grad_b, state_b)
    grad_k = multiply('...hts,...thd->...shd', attend, query_part) + weights * carried
    grad_v = multiply('...hts,...thv->...shv', mix_weights, grad_b) + weights * multiply('...shd,...hdv->...shv', key_part, later_b)
    own_term = lax.optimization_barrier(jnp.sum(scores * decay_mat * pushed, axis=-2)) + reach_fade * jnp.swapaxes(lax.optimization_barrier(jnp.sum(key_part.astype(jnp.float32) * carried, axis=-1)), -1, -2)
    grad_in = own_term * ingate * (1.0 - ingate)
    lift_term = jnp.swapaxes(lax.optimization_barrier(jnp.sum(grad_hidden * hidden, axis=-1)), -1, -2) - ingate * own_term
    return (grad_q, grad_k, grad_v, grad_in, lift_term)

def tail_cumsum(values_in):
    return jnp.flip(jnp.cumsum(jnp.flip(values_in, -1), axis=-1), -1)

def to_blocks(array_in):
    first = array_in[0].reshape((N_CTX, CH) + array_in.shape[2:])
    second = array_in[1].reshape((N_CTX, CH) + array_in.shape[2:])[::-1]
    return jnp.concatenate((first, second), axis=0)

def from_blocks(array_in):
    first = array_in[:N_CTX].reshape((HALF,) + array_in.shape[2:])
    second = array_in[N_CTX:][::-1].reshape((HALF,) + array_in.shape[2:])
    return jnp.stack((first, second), axis=0)

def gates_to_blocks(array_in):
    first = jnp.transpose(array_in[0].reshape(H, N_CTX, CH), (1, 0, 2))
    second = jnp.transpose(array_in[1].reshape(H, N_CTX, CH), (1, 0, 2))[::-1]
    return jnp.concatenate((first, second), axis=0)

def gates_from_blocks(array_in):
    first = jnp.transpose(array_in[:N_CTX], (1, 0, 2)).reshape(H, HALF)
    second = jnp.transpose(array_in[N_CTX:][::-1], (1, 0, 2)).reshape(H, HALF)
    return jnp.stack((first, second), axis=0)

def reference(queries, key_vectors, value_vectors, out_grad, forget_logits, input_logits, norm_gain):
    gain_rows = norm_gain.astype(jnp.float32).reshape(H, DV)
    block_count = 2 * N_CTX

    def forward(carry_state, piece_data):
        key_part, value_part, forget_part, input_part = piece_data
        forget_logit, ingate, cum_log, fade_total, decay_mat, reach_fade = gate_terms(forget_part, input_part)
        write_term = block_write(key_part, value_part, ingate, reach_fade)
        return (jnp.exp(fade_total)[:, None, None] * carry_state + write_term, carry_state)

    def backward(carry_in, piece_data):
        later_state, later_sum = carry_in
        query_part, key_part, value_part, grad_part, forget_part, input_part, state_in = piece_data
        forget_logit, ingate, cum_log, fade_total, decay_mat, reach_fade = gate_terms(forget_part, input_part)
        scores, mix_weights, state_b, hidden, early_fade = block_read(query_part, key_part, value_part, ingate, cum_log, decay_mat, state_in)
        grad_hidden, grad_b, normed, back_write = norm_back(hidden, grad_part, gain_rows, early_fade, query_part)
        grad_q, grad_k, grad_v, grad_in, lift_term = block_grads(query_part, key_part, value_part, ingate, reach_fade, decay_mat, early_fade, scores, mix_weights, state_b, hidden, grad_hidden, grad_b, later_state)
        tail_sum = tail_cumsum(lift_term)
        grad_f = (tail_sum + later_sum[:, None]) * jax.nn.sigmoid(-forget_logit)
        gain_part = lax.optimization_barrier(jnp.sum(grad_part.astype(jnp.float32) * normed, axis=0))
        next_state = jnp.exp(fade_total)[:, None, None] * later_state + back_write
        next_sum = later_sum + tail_sum[:, 0]
        outputs = (grad_q.astype(jnp.bfloat16), grad_k.astype(jnp.bfloat16), grad_v.astype(jnp.bfloat16), grad_f, grad_in, gain_part)
        return ((next_state, next_sum), outputs)

    def one_sequence(sequence_data):
        query_seq, key_seq, value_seq, grad_seq, forget_seq, input_seq = sequence_data
        query_part = to_blocks(query_seq).reshape(block_count, CH, H, DK)
        key_part = to_blocks(key_seq).reshape(block_count, CH, H, DK)
        value_part = to_blocks(value_seq).reshape(block_count, CH, H, DV)
        grad_part = to_blocks(grad_seq).reshape(block_count, CH, H, DV)
        forget_part = gates_to_blocks(forget_seq)
        input_part = gates_to_blocks(input_seq)
        zero_state = jnp.zeros((H, DK, DV), jnp.float32)
        unused, states = lax.scan(forward, zero_state, (key_part, value_part, forget_part, input_part))
        start_carry = (zero_state, jnp.zeros((H,), jnp.float32))
        unused_two, results = lax.scan(backward, start_carry, (query_part, key_part, value_part, grad_part, forget_part, input_part, states), reverse=True)
        grad_q, grad_k, grad_v, grad_f, grad_in, gain_part = results
        return (from_blocks(grad_q.reshape(block_count, CH, H * DK)), from_blocks(grad_k.reshape(block_count, CH, H * DK)), from_blocks(grad_v.reshape(block_count, CH, H * DV)), gates_from_blocks(grad_f), gates_from_blocks(grad_in), lax.optimization_barrier(jnp.sum(gain_part, axis=0)))
    grad_queries, grad_keys, grad_values, grad_forget, grad_input, gain_parts = lax.map(one_sequence, (queries, key_vectors, value_vectors, out_grad, forget_logits, input_logits))
    grad_gain = lax.optimization_barrier(jnp.sum(gain_parts, axis=0)).reshape(H * DV)
    return (grad_queries, grad_keys, grad_values, grad_forget, grad_input, grad_gain)
```

```python
import functools

import jax
import jax.numpy as jnp
from jax import lax
from jax.experimental import pallas as pl
from jax.experimental.pallas import tpu as pltpu
from jax.sharding import PartitionSpec as P

F32 = jnp.float32
BF16 = jnp.bfloat16
MESH = pl.DeviceIdType.MESH
HEADS = 4
CUM, ING, REACH, EARLY, WEIGHT = range(5)


def dot(left, right, left_dim, right_dim):
    return lax.dot_general(
        left, right, (((left_dim,), (right_dim,)), ((), ())), preferred_element_type=F32
    )


def twice(row):
    return jnp.concatenate([row, row], axis=1)


def kernel(
    rows_y,
    count_dp,
    q_ref,
    k_ref,
    v_ref,
    g_ref,
    f_ref,
    i_ref,
    gain_ref,
    gq_ref,
    gk_ref,
    gv_ref,
    gf_ref,
    gi_ref,
    gg_ref,
    s_kv,
    r_kv,
    s_qg,
    r_qg,
    s_gate,
    r_gate,
    s_fade,
    r_fade,
    cols,
    cum_rows,
    ing_rows,
    fade_blk,
    writes,
    totals,
    slices,
    s_state,
    r_state,
    state_b,
    scores_d,
    decay_i,
    mix_b,
    hidden_s,
    grad_b,
    ghh_cols,
    own_cols,
    s_q,
    r_q,
    s_out,
    r_out,
    s_lift,
    r_lift,
    s_fin,
    r_fin,
    s_g1,
    r_g1,
    s_g2,
    r_g2,
    s_g3,
    r_g3,
    x_ss,
    x_rs,
    y_ss,
    y_rs,
    d_ss,
    d_rs,
):
    me = lax.axis_index("ctx")
    my_dp = lax.axis_index("dp")
    my_x = lax.rem(me, HEADS)
    my_y = lax.div(me, HEADS)
    block = q_ref.shape[2]
    dk = q_ref.shape[3] // HEADS
    dv = v_ref.shape[3] // HEADS
    part = dk // rows_y

    def x_peer(step):
        return lax.rem(my_x + step, HEADS)

    def y_peer(step):
        return lax.rem(my_y + step, rows_y)

    def d_peer(step):
        return lax.rem(my_dp + step, count_dp)

    def to_x(step):
        return {"ctx": my_y * HEADS + x_peer(step)}

    def to_y(step):
        return {"ctx": y_peer(step) * HEADS + my_x}

    def to_d(step):
        return {"dp": d_peer(step)}

    started = []

    def send(src, dst, ss, rs, where):
        copy = pltpu.make_async_remote_copy(
            src_ref=src, dst_ref=dst, send_sem=ss, recv_sem=rs, device_id=where, device_id_type=MESH
        )
        copy.start()
        started.append(copy)
        return copy

    def x_send(kind, source, target):
        return [
            send(source(step), target, x_ss.at[kind, step - 1], x_rs.at[kind, step - 1], to_x(step))
            for step in range(1, HEADS)
        ]

    def y_send(kind, source, target):
        return [
            send(source(step), target, y_ss.at[kind, step - 1], y_rs.at[kind, step - 1], to_y(step))
            for step in range(1, rows_y)
        ]

    def arrive(copies):
        for copy in copies:
            copy.wait_recv()

    barrier = pltpu.get_barrier_semaphore()
    peers = (
        [to_x(s) for s in range(1, HEADS)]
        + [to_y(s) for s in range(1, rows_y)]
        + [to_d(s) for s in range(1, count_dp)]
    )
    for peer in peers:
        pl.semaphore_signal(barrier, inc=1, device_id=peer, device_id_type=MESH)

    lane8 = lax.broadcasted_iota(jnp.int32, (8, 128), 1)
    row8 = lax.broadcasted_iota(jnp.int32, (8, 128), 0)
    forget = jnp.concatenate([f_ref[0, 0], f_ref[0, 1]], axis=0).astype(F32)
    ingate_l = jnp.concatenate([i_ref[0, 0], i_ref[0, 1]], axis=0).astype(F32)
    logsig = -jnp.log1p(jnp.exp(-forget))
    ing_own = 1.0 / (1.0 + jnp.exp(-ingate_l))
    packed = jnp.concatenate([logsig, ing_own], axis=1)
    cum = packed
    hop = 1
    while hop < block:
        cum = cum + jnp.where(
            (lane8 >= hop) & (lane8 < block), pltpu.roll(cum, hop, axis=1), 0.0
        )
        hop *= 2
    s_gate[...] = cum
    r_gate[my_x] = cum

    for leg in range(2):
        for head in range(HEADS):
            s_kv[head, leg, :, :dk] = k_ref[0, leg, :, head * dk : (head + 1) * dk].astype(F32)
            s_kv[head, leg, :, dk:] = v_ref[0, leg, :, head * dv : (head + 1) * dv].astype(F32)

    pl.semaphore_wait(barrier, len(peers))
    gate_in = x_send(0, lambda step: s_gate, r_gate.at[my_x])
    kv_in = [
        x_send(1 + leg, lambda step, leg=leg: s_kv.at[x_peer(step), leg], r_kv.at[my_x, leg])
        for leg in range(2)
    ]
    for leg in range(2):
        r_kv[my_x, leg] = s_kv[my_x, leg]
        for head in range(HEADS):
            s_qg[head, leg, :, :dk] = q_ref[0, leg, :, head * dk : (head + 1) * dk].astype(F32)
            s_qg[head, leg, :, dk:] = g_ref[0, leg, :, head * dv : (head + 1) * dv].astype(F32)
        r_qg[my_x, leg] = s_qg[my_x, leg]

    arrive(gate_in)
    gates = jnp.concatenate(
        [
            r_gate[source, pl.ds(leg * HEADS + my_x, 1), :]
            for leg in range(2)
            for source in range(HEADS)
        ],
        axis=0,
    )
    total_log = gates[:, block - 1 : block]
    ingate = pltpu.roll(gates, block, axis=1)
    reach = jnp.exp(total_log - gates)
    cum_rows[...] = gates
    ing_rows[...] = ingate
    fade_blk[...] = jnp.broadcast_to(jnp.exp(total_log), (8, 128))
    stacked = jnp.concatenate(
        [gates, ingate, reach, jnp.exp(gates), ingate * reach, jnp.zeros((88, 128), F32)], axis=0
    )
    cols[...] = jnp.transpose(stacked)
    leg_sum = [
        jnp.sum(total_log[leg * HEADS : (leg + 1) * HEADS], axis=0, keepdims=True)
        for leg in range(2)
    ]
    row_fade = jnp.exp(jnp.where(row8 == 0, leg_sum[0], leg_sum[1]))
    s_fade[...] = row_fade
    r_fade[my_y] = row_fade
    fade_in = y_send(0, lambda step: s_fade, r_fade.at[my_y])

    def col(kind, index):
        at = kind * 8 + index
        return cols[0:block, at : at + 1]

    def fade_of(index):
        return twice(fade_blk[index : index + 1, :])

    def key_of(leg, source):
        return r_kv[source, leg, :, :dk].astype(BF16)

    def value_of(leg, source):
        return r_kv[source, leg, :, dk:].astype(BF16)

    def query_of(leg, source):
        return r_qg[source, leg, :, :dk].astype(BF16)

    onward = list(range(HEADS))
    order = [[onward, onward[::-1]], [onward[::-1], onward]]

    def send_total(phase, leg):
        path = order[phase][leg]
        total = writes[phase, leg, path[0]]
        for source in path[1:]:
            total = fade_of(leg * HEADS + source) * total + writes[phase, leg, source]
        totals[phase, leg] = total.reshape(rows_y, part, dv)
        slices[phase, leg, my_y] = totals[phase, leg, my_y]
        return y_send(
            3 + 4 * phase + 2 * leg,
            lambda step: totals.at[phase, leg, y_peer(step)],
            slices.at[phase, leg, my_y],
        )

    def scan_rows(phase, leg, path, state):
        for row in path:
            s_state[phase, leg, row] = state
            state = twice(r_fade[row, leg : leg + 1, :]) * state + slices[phase, leg, row]
        r_state[phase, leg, my_y] = s_state[phase, leg, my_y]
        copies = y_send(
            4 + 4 * phase + 2 * leg,
            lambda step: s_state.at[phase, leg, y_peer(step)],
            r_state.at[phase, leg, my_y],
        )
        return state, copies

    slices_in = [[None, None], [None, None]]
    states_in = [[None, None], [None, None]]
    for leg in range(2):
        arrive(kv_in[leg])
        for source in range(HEADS):
            value = r_kv[source, leg, :, dk:]
            scaled = (value * col(WEIGHT, leg * HEADS + source)).astype(BF16)
            writes[0, leg, source] = dot(key_of(leg, source), scaled, 0, 0)
        slices_in[0][leg] = send_total(0, leg)

    qg_in = [
        x_send(3 + leg, lambda step, leg=leg: s_qg.at[x_peer(step), leg], r_qg.at[my_x, leg])
        for leg in range(2)
    ]

    row_id = lax.broadcasted_iota(jnp.int32, (block, block), 0)
    col_id = lax.broadcasted_iota(jnp.int32, (block, block), 1)
    causal = col_id >= row_id

    arrive(fade_in)
    upward = list(range(rows_y))
    zero_state = jnp.zeros((part, dv), F32)
    arrive(slices_in[0][0])
    through, states_in[0][0] = scan_rows(0, 0, upward, zero_state)
    arrive(slices_in[0][1])
    _, states_in[0][1] = scan_rows(0, 1, upward[::-1], through)

    for leg in range(2):
        arrive(qg_in[leg])
        for source in range(HEADS):
            index = leg * HEADS + source
            scores = dot(key_of(leg, source), query_of(leg, source), 1, 1)
            spread = cum_rows[index : index + 1, 0:block] - col(CUM, index)
            decay = jnp.where(causal, jnp.exp(jnp.where(causal, spread, 0.0)), 0.0)
            weighted = scores * decay
            mix = (weighted * col(ING, index)).astype(BF16)
            scores_d[index] = weighted
            decay_i[index] = decay * col(ING, index)
            mix_b[index] = mix
            hidden_s[index] = dot(mix, value_of(leg, source), 0, 0)

    lane_b = lax.broadcasted_iota(jnp.int32, (block, 128), 1)
    gain_all = gain_ref[...].astype(F32)
    head_id = lax.broadcasted_iota(jnp.int32, gain_all.shape, 0)
    gain_row = jnp.sum(jnp.where(head_id == my_x, gain_all, 0.0), axis=0, keepdims=True)
    gain_sum = jnp.zeros((8, dv), F32)
    ghh = jnp.zeros((block, 128), F32)
    for leg in range(2):
        arrive(states_in[0][leg])
        state = r_state[0, leg].reshape(dk, dv)
        for source in order[0][leg]:
            index = leg * HEADS + source
            query = query_of(leg, source)
            early = col(EARLY, index)
            rounded = state.astype(BF16)
            state_b[index] = rounded
            hidden = hidden_s[index] + early * dot(query, rounded, 1, 0)
            inv_rms = lax.rsqrt(jnp.mean(hidden * hidden, axis=1, keepdims=True) + 1e-05)
            normed = hidden * inv_rms
            out_grad = r_qg[source, leg, :, dk:]
            pushed = out_grad * gain_row
            center = jnp.mean(pushed * normed, axis=1, keepdims=True)
            grad_hidden = inv_rms * (pushed - normed * center)
            grad_b[index] = grad_hidden.astype(BF16)
            lifted = (grad_hidden * early).astype(BF16)
            writes[1, leg, source] = dot(query, lifted, 0, 0)
            gain_sum = gain_sum + jnp.sum(
                (out_grad * normed).reshape(block // 8, 8, dv), axis=0
            )
            ghh = jnp.where(
                lane_b == index, jnp.sum(grad_hidden * hidden, axis=1, keepdims=True), ghh
            )
            state = fade_of(index) * state + writes[0, leg, source]
    ghh_cols[...] = ghh
    slices_in[1][1] = send_total(1, 1)
    slices_in[1][0] = send_total(1, 0)
    s_g1[...] = gain_sum
    r_g1[my_y] = gain_sum
    gain1_in = y_send(2, lambda step: s_g1, r_g1.at[my_y])

    own_sum = jnp.zeros((block, 128), F32)
    grad_q_in = [None, None]
    for leg in (1, 0):
        for source in range(HEADS):
            index = leg * HEADS + source
            grad = grad_b[index]
            key = key_of(leg, source)
            pushed_mix = dot(value_of(leg, source), grad, 1, 1)
            attend = (pushed_mix * decay_i[index]).astype(BF16)
            own_sum = jnp.where(
                lane_b == index,
                jnp.sum(scores_d[index] * pushed_mix, axis=1, keepdims=True),
                own_sum,
            )
            s_q[source, leg] = dot(attend, key, 0, 0) + col(EARLY, index) * dot(
                grad, state_b[index], 1, 1
            )
            s_out[source, leg, :, :dk] = dot(attend, query_of(leg, source), 1, 0)
            s_out[source, leg, :, dk:] = dot(mix_b[index], grad, 1, 0)
        r_q[my_x, leg] = s_q[my_x, leg]
        grad_q_in[leg] = x_send(
            5 + leg, lambda step, leg=leg: s_q.at[x_peer(step), leg], r_q.at[my_x, leg]
        )
    own_cols[...] = own_sum

    arrive(slices_in[1][1])
    through, states_in[1][1] = scan_rows(1, 1, upward, zero_state)
    arrive(slices_in[1][0])
    _, states_in[1][0] = scan_rows(1, 0, upward[::-1], through)

    arrive(gain1_in)
    gain_sum = r_g1[0]
    for row in range(1, rows_y):
        gain_sum = gain_sum + r_g1[row]
    gain_sum = jnp.sum(gain_sum, axis=0, keepdims=True)
    gain_sum = jnp.concatenate([gain_sum[:, :128], gain_sum[:, 128:]], axis=0)
    s_g2[...] = gain_sum
    r_g2[my_dp] = gain_sum
    gain2_in = [
        send(s_g2, r_g2.at[my_dp], d_ss.at[step - 1], d_rs.at[step - 1], to_d(step))
        for step in range(1, count_dp)
    ]

    own_sum = own_cols[...]
    out_in = [None, None]
    for leg in (1, 0):
        arrive(states_in[1][leg])
        state = r_state[1, leg].reshape(dk, dv)
        for source in order[1][leg]:
            index = leg * HEADS + source
            rounded = state.astype(BF16)
            weight = col(WEIGHT, index)
            carried = dot(value_of(leg, source), rounded, 1, 1)
            s_out[source, leg, :, :dk] = s_out[source, leg, :, :dk] + weight * carried
            s_out[source, leg, :, dk:] = s_out[source, leg, :, dk:] + weight * dot(
                key_of(leg, source), rounded, 1, 0
            )
            extra = col(REACH, index) * jnp.sum(
                r_kv[source, leg, :, :dk] * carried, axis=1, keepdims=True
            )
            own_sum = jnp.where(lane_b == index, own_sum + extra, own_sum)
            state = fade_of(index) * state + writes[1, leg, source]
        r_out[my_x, leg] = s_out[my_x, leg]
        out_in[leg] = x_send(
            7 + leg, lambda step, leg=leg: s_out.at[x_peer(step), leg], r_out.at[my_x, leg]
        )

    turned = jnp.transpose(jnp.concatenate([own_sum, ghh_cols[...]], axis=0))[0:8]
    ing = ing_rows[...]
    lift = pltpu.roll(turned, block, axis=1) - ing * turned
    tail = jnp.where(lane8 < block, lift, 0.0)
    hop = 1
    while hop < block:
        tail = tail + pltpu.roll(tail, 128 - hop, axis=1) * (lane8 < block - hop).astype(F32)
        hop *= 2
    sums = jnp.broadcast_to(tail[:, 0:1], (8, 128))
    leg_total = [
        jnp.sum(sums[leg * HEADS : (leg + 1) * HEADS], axis=0, keepdims=True) for leg in range(2)
    ]
    tile = jnp.where(row8 == 0, leg_total[0], leg_total[1])
    s_lift[...] = tile
    r_lift[my_y] = tile
    lift_in = y_send(1, lambda step: s_lift, r_lift.at[my_y])

    arrive(gain2_in)
    gain_sum = r_g2[0]
    for row in range(1, count_dp):
        gain_sum = gain_sum + r_g2[row]
    s_g3[...] = gain_sum
    r_g3[my_x] = gain_sum
    gain3_in = x_send(10, lambda step: s_g3, r_g3.at[my_x])

    later_rows = [None] * 8
    zero_row = jnp.zeros((1, 128), F32)
    run = zero_row
    for source in range(HEADS):
        later_rows[HEADS + source] = run
        run = run + sums[HEADS + source : HEADS + source + 1]
    run = zero_row
    for source in reversed(range(HEADS)):
        later_rows[source] = run
        run = run + sums[source : source + 1]
    later = jnp.concatenate(later_rows, axis=0)

    arrive(lift_in)
    after_out = zero_row
    after_home = zero_row
    for row in range(rows_y):
        home = r_lift[row, 1:2, :]
        after_out = after_out + home + jnp.where(row > my_y, r_lift[row, 0:1, :], 0.0)
        after_home = after_home + jnp.where(row < my_y, home, 0.0)
    later = later + jnp.where(row8 < HEADS, after_out, after_home)
    fin = jnp.where(
        lane8 < block,
        turned * ing * (1.0 - ing),
        pltpu.roll(tail + later, block, axis=1),
    )
    s_fin[...] = fin
    r_fin[my_x] = fin
    fin_in = x_send(9, lambda step: s_fin, r_fin.at[my_x])

    for leg in (1, 0):
        arrive(grad_q_in[leg])
        for head in range(HEADS):
            gq_ref[0, leg, :, head * dk : (head + 1) * dk] = r_q[head, leg].astype(BF16)
    for leg in (1, 0):
        arrive(out_in[leg])
        for head in range(HEADS):
            gk_ref[0, leg, :, head * dk : (head + 1) * dk] = r_out[head, leg, :, :dk].astype(BF16)
            gv_ref[0, leg, :, head * dv : (head + 1) * dv] = r_out[head, leg, :, dk:].astype(BF16)
    arrive(gain3_in)
    for head in range(HEADS):
        gg_ref[2 * head : 2 * head + 2, :] = r_g3[head]
    arrive(fin_in)
    for leg in range(2):
        rows = jnp.concatenate(
            [r_fin[head, pl.ds(leg * HEADS + my_x, 1), :] for head in range(HEADS)], axis=0
        )
        slope = 1.0 / (1.0 + jnp.exp(f_ref[0, leg].astype(F32)))
        gi_ref[0, leg] = rows[:, :block]
        gf_ref[0, leg] = rows[:, block:] * slope
    for copy in started:
        copy.wait_send()


def shards(rows_y, count_dp, queries, keys, values, out_grad, forget, inputs, gain):
    block = queries.shape[2]
    dk = queries.shape[3] // HEADS
    dv = values.shape[3] // HEADS
    part = dk // rows_y
    vmem = pltpu.VMEM
    scratch = [
        vmem((HEADS, 2, block, dk + dv), F32),
        vmem((HEADS, 2, block, dk + dv), F32),
        vmem((HEADS, 2, block, dk + dv), F32),
        vmem((HEADS, 2, block, dk + dv), F32),
        vmem((8, 128), F32),
        vmem((HEADS, 8, 128), F32),
        vmem((8, 128), F32),
        vmem((rows_y, 8, 128), F32),
        vmem((128, 128), F32),
        vmem((8, 128), F32),
        vmem((8, 128), F32),
        vmem((8, 128), F32),
        vmem((2, 2, HEADS, dk, dv), F32),
        vmem((2, 2, rows_y, part, dv), F32),
        vmem((2, 2, rows_y, part, dv), F32),
        vmem((2, 2, rows_y, part, dv), F32),
        vmem((2, 2, rows_y, part, dv), F32),
        vmem((8, dk, dv), BF16),
        vmem((8, block, block), F32),
        vmem((8, block, block), F32),
        vmem((8, block, block), BF16),
        vmem((8, block, dv), F32),
        vmem((8, block, dv), BF16),
        vmem((block, 128), F32),
        vmem((block, 128), F32),
        vmem((HEADS, 2, block, dk), F32),
        vmem((HEADS, 2, block, dk), F32),
        vmem((HEADS, 2, block, dk + dv), F32),
        vmem((HEADS, 2, block, dk + dv), F32),
        vmem((8, 128), F32),
        vmem((rows_y, 8, 128), F32),
        vmem((8, 128), F32),
        vmem((HEADS, 8, 128), F32),
        vmem((8, dv), F32),
        vmem((rows_y, 8, dv), F32),
        vmem((2, 128), F32),
        vmem((count_dp, 2, 128), F32),
        vmem((2, 128), F32),
        vmem((HEADS, 2, 128), F32),
        pltpu.SemaphoreType.DMA((11, HEADS - 1)),
        pltpu.SemaphoreType.DMA((11, HEADS - 1)),
        pltpu.SemaphoreType.DMA((11, rows_y - 1)),
        pltpu.SemaphoreType.DMA((11, rows_y - 1)),
        pltpu.SemaphoreType.DMA((max(count_dp - 1, 1),)),
        pltpu.SemaphoreType.DMA((max(count_dp - 1, 1),)),
    ]
    spec = pl.BlockSpec(memory_space=pltpu.VMEM)
    outs = pl.pallas_call(
        functools.partial(kernel, rows_y, count_dp),
        out_shape=(
            jax.ShapeDtypeStruct(queries.shape, BF16),
            jax.ShapeDtypeStruct(keys.shape, BF16),
            jax.ShapeDtypeStruct(values.shape, BF16),
            jax.ShapeDtypeStruct(forget.shape, F32),
            jax.ShapeDtypeStruct(inputs.shape, F32),
            jax.ShapeDtypeStruct((8, 128), F32),
        ),
        in_specs=[spec] * 7,
        out_specs=(spec,) * 6,
        scratch_shapes=scratch,
        compiler_params=pltpu.CompilerParams(
            collective_id=0, has_side_effects=True, vmem_limit_bytes=48 * 1024 * 1024
        ),
        name="mlstm_back",
    )(queries, keys, values, out_grad, forget, inputs, gain.reshape(HEADS, -1))
    return outs[:5] + (outs[5].reshape(-1),)


def solution(mesh):
    return jax.shard_map(
        functools.partial(shards, mesh.shape["ctx"] // HEADS, mesh.shape["dp"]),
        mesh=mesh,
        in_specs=(
            P("dp", None, "ctx", None),
            P("dp", None, "ctx", None),
            P("dp", None, "ctx", None),
            P("dp", None, "ctx", None),
            P("dp", None, None, "ctx"),
            P("dp", None, None, "ctx"),
            P(),
        ),
        out_specs=(
            P("dp", None, "ctx", None),
            P("dp", None, "ctx", None),
            P("dp", None, "ctx", None),
            P("dp", None, None, "ctx"),
            P("dp", None, None, "ctx"),
            P(),
        ),
        check_vma=False,
    )
```

```python
import functools

import jax
import jax.numpy as jnp
from jax import lax
from jax.experimental import pallas as pl
from jax.experimental.pallas import tpu as pltpu
from jax.sharding import PartitionSpec as P

F32 = jnp.float32
BF16 = jnp.bfloat16
MESH = pl.DeviceIdType.MESH
HEADS = 4
CUM, ING, REACH, EARLY, WEIGHT = range(5)


def dot(left, right, left_dim, right_dim):
    return lax.dot_general(
        left, right, (((left_dim,), (right_dim,)), ((), ())), preferred_element_type=F32
    )


def twice(row):
    return jnp.concatenate([row, row], axis=1)


def kernel(
    rows_y,
    count_dp,
    q_hbm,
    k_hbm,
    v_hbm,
    g_hbm,
    f_hbm,
    i_hbm,
    gain_hbm,
    gq_ref,
    gk_ref,
    gv_ref,
    gf_ref,
    gi_ref,
    gg_ref,
    q_ref,
    k_ref,
    v_ref,
    g_ref,
    f_ref,
    i_ref,
    gain_ref,
    in_sem,
    s_kv,
    r_kv,
    s_qg,
    r_qg,
    s_gate,
    r_gate,
    s_fade,
    r_fade,
    cols,
    cum_rows,
    ing_rows,
    fade_blk,
    writes,
    totals,
    slices,
    s_state,
    r_state,
    state_b,
    scores_d,
    decay_i,
    mix_b,
    hidden_s,
    grad_b,
    ghh_cols,
    own_cols,
    s_q,
    r_q,
    s_out,
    r_out,
    s_lift,
    r_lift,
    s_fin,
    r_fin,
    s_g1,
    r_g1,
    s_g2,
    r_g2,
    s_g3,
    r_g3,
    x_ss,
    x_rs,
    y_ss,
    y_rs,
    d_ss,
    d_rs,
    g1_ss,
    g1_rs,
    g3_ss,
    g3_rs,
    ready,
):
    inputs = [
        pltpu.make_async_copy(src, dst, in_sem.at[number])
        for number, (src, dst) in enumerate(
            [
                (f_hbm, f_ref),
                (i_hbm, i_ref),
                (k_hbm, k_ref),
                (v_hbm, v_ref),
                (q_hbm, q_ref),
                (g_hbm, g_ref),
                (gain_hbm, gain_ref),
            ]
        )
    ]
    for copy in inputs:
        copy.start()
    me = lax.axis_index("ctx")
    my_dp = lax.axis_index("dp")
    my_x = lax.rem(me, HEADS)
    my_y = lax.div(me, HEADS)
    block = q_ref.shape[2]
    dk = q_ref.shape[3] // HEADS
    dv = v_ref.shape[3] // HEADS
    part = dk // rows_y

    def x_peer(step):
        return lax.rem(my_x + step, HEADS)

    def y_peer(step):
        return lax.rem(my_y + step, rows_y)

    def d_peer(step):
        return lax.rem(my_dp + step, count_dp)

    def to_x(step):
        return {"ctx": my_y * HEADS + x_peer(step)}

    def to_y(step):
        return {"ctx": y_peer(step) * HEADS + my_x}

    def to_d(step):
        return {"dp": d_peer(step)}

    started = []

    def send(src, dst, ss, rs, where):
        copy = pltpu.make_async_remote_copy(
            src_ref=src, dst_ref=dst, send_sem=ss, recv_sem=rs, device_id=where, device_id_type=MESH
        )
        copy.start()
        started.append(copy)
        return copy

    def x_send(kind, source, target):
        return [
            send(source(step), target, x_ss.at[kind, step - 1], x_rs.at[kind, step - 1], to_x(step))
            for step in range(1, HEADS)
        ]

    def y_send(kind, source, target):
        return [
            send(source(step), target, y_ss.at[kind, step - 1], y_rs.at[kind, step - 1], to_y(step))
            for step in range(1, rows_y)
        ]

    def arrive(copies):
        for copy in copies:
            copy.wait_recv()

    is_gate = my_x == my_y
    barrier = pltpu.get_barrier_semaphore()
    plane = HEADS - 1 + rows_y - 1

    def signal(sem, where):
        pl.semaphore_signal(sem, inc=1, device_id=where, device_id_type=MESH)

    for step in range(1, HEADS):

        @pl.when(x_peer(step) != my_y)
        def _():
            signal(barrier, to_x(step))

    for step in range(1, rows_y):

        @pl.when(y_peer(step) != my_x)
        def _():
            signal(barrier, to_y(step))

    @pl.when(is_gate)
    def _():
        for step in range(1, count_dp):
            signal(barrier, to_d(step))


    lane8 = lax.broadcasted_iota(jnp.int32, (8, 128), 1)
    row8 = lax.broadcasted_iota(jnp.int32, (8, 128), 0)
    inputs[0].wait()
    inputs[1].wait()
    forget = jnp.concatenate([f_ref[0, 0], f_ref[0, 1]], axis=0).astype(F32)
    ingate_l = jnp.concatenate([i_ref[0, 0], i_ref[0, 1]], axis=0).astype(F32)
    logsig = -jnp.log1p(jnp.exp(-forget))
    ing_own = 1.0 / (1.0 + jnp.exp(-ingate_l))
    packed = jnp.concatenate([logsig, ing_own], axis=1)
    cum = packed
    hop = 1
    while hop < block:
        cum = cum + jnp.where(
            (lane8 >= hop) & (lane8 < block), pltpu.roll(cum, hop, axis=1), 0.0
        )
        hop *= 2
    s_gate[...] = cum
    r_gate[my_x] = cum

    inputs[2].wait()
    inputs[3].wait()
    for leg in range(2):
        for head in range(HEADS):
            s_kv[head, leg, :, :dk] = k_ref[0, leg, :, head * dk : (head + 1) * dk].astype(F32)
            s_kv[head, leg, :, dk:] = v_ref[0, leg, :, head * dv : (head + 1) * dv].astype(F32)

    @pl.when(jnp.logical_not(is_gate))
    def _():
        pl.semaphore_wait(barrier, plane)

        @pl.when((my_y < HEADS) & (my_x == lax.rem(my_y + 1, HEADS)))
        def _():
            signal(ready, {"ctx": my_y * HEADS + my_y})

        @pl.when(my_y == lax.rem(my_x + 1, rows_y))
        def _():
            signal(ready, {"ctx": my_x * HEADS + my_x})

    @pl.when(is_gate)
    def _():
        pl.semaphore_wait(ready, 2)

    gate_in = x_send(0, lambda step: s_gate, r_gate.at[my_x])
    kv_in = [
        x_send(1 + leg, lambda step, leg=leg: s_kv.at[x_peer(step), leg], r_kv.at[my_x, leg])
        for leg in range(2)
    ]
    for copy in inputs[4:]:
        copy.wait()
    for leg in range(2):
        r_kv[my_x, leg] = s_kv[my_x, leg]
        for head in range(HEADS):
            s_qg[head, leg, :, :dk] = q_ref[0, leg, :, head * dk : (head + 1) * dk].astype(F32)
            s_qg[head, leg, :, dk:] = g_ref[0, leg, :, head * dv : (head + 1) * dv].astype(F32)
        r_qg[my_x, leg] = s_qg[my_x, leg]

    arrive(gate_in)
    gates = jnp.concatenate(
        [
            r_gate[source, pl.ds(leg * HEADS + my_x, 1), :]
            for leg in range(2)
            for source in range(HEADS)
        ],
        axis=0,
    )
    total_log = gates[:, block - 1 : block]
    ingate = pltpu.roll(gates, block, axis=1)
    reach = jnp.exp(total_log - gates)
    cum_rows[...] = gates
    ing_rows[...] = ingate
    fade_blk[...] = jnp.broadcast_to(jnp.exp(total_log), (8, 128))
    stacked = jnp.concatenate(
        [gates, ingate, reach, jnp.exp(gates), ingate * reach, jnp.zeros((88, 128), F32)], axis=0
    )
    cols[...] = jnp.transpose(stacked)
    leg_sum = [
        jnp.sum(total_log[leg * HEADS : (leg + 1) * HEADS], axis=0, keepdims=True)
        for leg in range(2)
    ]
    row_fade = jnp.exp(jnp.where(row8 == 0, leg_sum[0], leg_sum[1]))
    s_fade[...] = row_fade
    r_fade[my_y] = row_fade
    fade_in = y_send(0, lambda step: s_fade, r_fade.at[my_y])

    def col(kind, index):
        at = kind * 8 + index
        return cols[0:block, at : at + 1]

    def fade_of(index):
        return twice(fade_blk[index : index + 1, :])

    def key_of(leg, source):
        return r_kv[source, leg, :, :dk].astype(BF16)

    def value_of(leg, source):
        return r_kv[source, leg, :, dk:].astype(BF16)

    def query_of(leg, source):
        return r_qg[source, leg, :, :dk].astype(BF16)

    onward = list(range(HEADS))
    order = [[onward, onward[::-1]], [onward[::-1], onward]]

    def send_total(phase, leg):
        path = order[phase][leg]
        total = writes[phase, leg, path[0]]
        for source in path[1:]:
            total = fade_of(leg * HEADS + source) * total + writes[phase, leg, source]
        totals[phase, leg] = total.reshape(rows_y, part, dv)
        slices[phase, leg, my_y] = totals[phase, leg, my_y]
        return y_send(
            3 + 4 * phase + 2 * leg,
            lambda step: totals.at[phase, leg, y_peer(step)],
            slices.at[phase, leg, my_y],
        )

    def scan_rows(phase, leg, path, state):
        for row in path:
            s_state[phase, leg, row] = state
            state = twice(r_fade[row, leg : leg + 1, :]) * state + slices[phase, leg, row]
        r_state[phase, leg, my_y] = s_state[phase, leg, my_y]
        copies = y_send(
            4 + 4 * phase + 2 * leg,
            lambda step: s_state.at[phase, leg, y_peer(step)],
            r_state.at[phase, leg, my_y],
        )
        return state, copies

    slices_in = [[None, None], [None, None]]
    states_in = [[None, None], [None, None]]
    for leg in range(2):
        arrive(kv_in[leg])
        for source in range(HEADS):
            value = r_kv[source, leg, :, dk:]
            scaled = (value * col(WEIGHT, leg * HEADS + source)).astype(BF16)
            writes[0, leg, source] = dot(key_of(leg, source), scaled, 0, 0)
        slices_in[0][leg] = send_total(0, leg)

    qg_in = [
        x_send(3 + leg, lambda step, leg=leg: s_qg.at[x_peer(step), leg], r_qg.at[my_x, leg])
        for leg in range(2)
    ]

    row_id = lax.broadcasted_iota(jnp.int32, (block, block), 0)
    col_id = lax.broadcasted_iota(jnp.int32, (block, block), 1)
    causal = col_id >= row_id

    arrive(fade_in)
    upward = list(range(rows_y))
    zero_state = jnp.zeros((part, dv), F32)
    arrive(slices_in[0][0])
    through, states_in[0][0] = scan_rows(0, 0, upward, zero_state)
    arrive(slices_in[0][1])
    _, states_in[0][1] = scan_rows(0, 1, upward[::-1], through)

    for leg in range(2):
        arrive(qg_in[leg])
        for source in range(HEADS):
            index = leg * HEADS + source
            scores = dot(key_of(leg, source), query_of(leg, source), 1, 1)
            spread = cum_rows[index : index + 1, 0:block] - col(CUM, index)
            decay = jnp.where(causal, jnp.exp(jnp.where(causal, spread, 0.0)), 0.0)
            weighted = scores * decay
            mix = (weighted * col(ING, index)).astype(BF16)
            scores_d[index] = weighted
            decay_i[index] = decay * col(ING, index)
            mix_b[index] = mix
            hidden_s[index] = dot(mix, value_of(leg, source), 0, 0)

    lane_b = lax.broadcasted_iota(jnp.int32, (block, 128), 1)
    gain_all = gain_ref[...].astype(F32)
    head_id = lax.broadcasted_iota(jnp.int32, gain_all.shape, 0)
    gain_row = jnp.concatenate(
        [
            jnp.sum(jnp.where(head_id == 2 * my_x + half, gain_all, 0.0), axis=0, keepdims=True)
            for half in range(2)
        ],
        axis=1,
    )
    gain_sum = jnp.zeros((8, dv), F32)
    ghh = jnp.zeros((block, 128), F32)
    for leg in range(2):
        arrive(states_in[0][leg])
        state = r_state[0, leg].reshape(dk, dv)
        for source in order[0][leg]:
            index = leg * HEADS + source
            query = query_of(leg, source)
            early = col(EARLY, index)
            rounded = state.astype(BF16)
            state_b[index] = rounded
            hidden = hidden_s[index] + early * dot(query, rounded, 1, 0)
            inv_rms = lax.rsqrt(jnp.mean(hidden * hidden, axis=1, keepdims=True) + 1e-05)
            normed = hidden * inv_rms
            out_grad = r_qg[source, leg, :, dk:]
            pushed = out_grad * gain_row
            center = jnp.mean(pushed * normed, axis=1, keepdims=True)
            grad_hidden = inv_rms * (pushed - normed * center)
            grad_b[index] = grad_hidden.astype(BF16)
            lifted = (grad_hidden * early).astype(BF16)
            writes[1, leg, source] = dot(query, lifted, 0, 0)
            gain_sum = gain_sum + jnp.sum(
                (out_grad * normed).reshape(block // 8, 8, dv), axis=0
            )
            ghh = jnp.where(
                lane_b == index, jnp.sum(grad_hidden * hidden, axis=1, keepdims=True), ghh
            )
            state = fade_of(index) * state + writes[0, leg, source]
    ghh_cols[...] = ghh
    slices_in[1][1] = send_total(1, 1)
    slices_in[1][0] = send_total(1, 0)
    gain_sum = jnp.sum(gain_sum, axis=0, keepdims=True)
    gain_sum = jnp.concatenate([gain_sum[:, :128], gain_sum[:, 128:]], axis=0)
    s_g1[...] = gain_sum
    r_g1[my_y] = gain_sum

    def remote(src, dst, ss, rs, where):
        return pltpu.make_async_remote_copy(
            src_ref=src, dst_ref=dst, send_sem=ss, recv_sem=rs, device_id=where, device_id_type=MESH
        )

    def gain1():
        gate = {"ctx": my_x * HEADS + my_x}
        return remote(s_g1, r_g1.at[my_y], g1_ss.at[0], g1_rs.at[my_y], gate)

    def gain2(step):
        return remote(s_g2, r_g2.at[my_dp], d_ss.at[step - 1], d_rs.at[step - 1], to_d(step))

    def gain3(step):
        where = {"ctx": lax.rem(me + step, HEADS * rows_y)}
        return remote(s_g3, r_g3.at[my_x], g3_ss.at[step - 1], g3_rs.at[my_x], where)

    @pl.when(jnp.logical_not(is_gate))
    def _():
        gain1().start()

    own_sum = jnp.zeros((block, 128), F32)
    grad_q_in = [None, None]
    for leg in (1, 0):
        for source in range(HEADS):
            index = leg * HEADS + source
            grad = grad_b[index]
            key = key_of(leg, source)
            pushed_mix = dot(value_of(leg, source), grad, 1, 1)
            attend = (pushed_mix * decay_i[index]).astype(BF16)
            own_sum = jnp.where(
                lane_b == index,
                jnp.sum(scores_d[index] * pushed_mix, axis=1, keepdims=True),
                own_sum,
            )
            s_q[source, leg] = dot(attend, key, 0, 0) + col(EARLY, index) * dot(
                grad, state_b[index], 1, 1
            )
            s_out[source, leg, :, :dk] = dot(attend, query_of(leg, source), 1, 0)
            s_out[source, leg, :, dk:] = dot(mix_b[index], grad, 1, 0)
        r_q[my_x, leg] = s_q[my_x, leg]
        grad_q_in[leg] = x_send(
            5 + leg, lambda step, leg=leg: s_q.at[x_peer(step), leg], r_q.at[my_x, leg]
        )
    own_cols[...] = own_sum

    arrive(slices_in[1][1])
    through, states_in[1][1] = scan_rows(1, 1, upward, zero_state)
    arrive(slices_in[1][0])
    _, states_in[1][0] = scan_rows(1, 0, upward[::-1], through)

    @pl.when(is_gate)
    def _():
        for step in range(1, rows_y):
            row = y_peer(step)
            remote(s_g1, r_g1.at[row], g1_ss.at[0], g1_rs.at[row], to_y(step)).wait_recv()
        gain_sum = r_g1[0]
        for row in range(1, rows_y):
            gain_sum = gain_sum + r_g1[row]
        s_g2[...] = gain_sum
        r_g2[my_dp] = gain_sum
        if count_dp > 1:
            pl.semaphore_wait(barrier, count_dp - 1)
        for step in range(1, count_dp):
            gain2(step).start()


    own_sum = own_cols[...]
    out_in = [None, None]
    for leg in (1, 0):
        arrive(states_in[1][leg])
        state = r_state[1, leg].reshape(dk, dv)
        for source in order[1][leg]:
            index = leg * HEADS + source
            rounded = state.astype(BF16)
            weight = col(WEIGHT, index)
            carried = dot(value_of(leg, source), rounded, 1, 1)
            s_out[source, leg, :, :dk] = s_out[source, leg, :, :dk] + weight * carried
            s_out[source, leg, :, dk:] = s_out[source, leg, :, dk:] + weight * dot(
                key_of(leg, source), rounded, 1, 0
            )
            extra = col(REACH, index) * jnp.sum(
                r_kv[source, leg, :, :dk] * carried, axis=1, keepdims=True
            )
            own_sum = jnp.where(lane_b == index, own_sum + extra, own_sum)
            state = fade_of(index) * state + writes[1, leg, source]
        r_out[my_x, leg] = s_out[my_x, leg]
        out_in[leg] = x_send(
            7 + leg, lambda step, leg=leg: s_out.at[x_peer(step), leg], r_out.at[my_x, leg]
        )

    turned = jnp.transpose(jnp.concatenate([own_sum, ghh_cols[...]], axis=0))[0:8]
    ing = ing_rows[...]
    lift = pltpu.roll(turned, block, axis=1) - ing * turned
    tail = jnp.where(lane8 < block, lift, 0.0)
    hop = 1
    while hop < block:
        tail = tail + pltpu.roll(tail, 128 - hop, axis=1) * (lane8 < block - hop).astype(F32)
        hop *= 2
    sums = jnp.broadcast_to(tail[:, 0:1], (8, 128))
    leg_total = [
        jnp.sum(sums[leg * HEADS : (leg + 1) * HEADS], axis=0, keepdims=True) for leg in range(2)
    ]
    tile = jnp.where(row8 == 0, leg_total[0], leg_total[1])
    s_lift[...] = tile
    r_lift[my_y] = tile
    lift_in = y_send(1, lambda step: s_lift, r_lift.at[my_y])

    later_rows = [None] * 8
    zero_row = jnp.zeros((1, 128), F32)
    run = zero_row
    for source in range(HEADS):
        later_rows[HEADS + source] = run
        run = run + sums[HEADS + source : HEADS + source + 1]
    run = zero_row
    for source in reversed(range(HEADS)):
        later_rows[source] = run
        run = run + sums[source : source + 1]
    later = jnp.concatenate(later_rows, axis=0)

    arrive(lift_in)
    after_out = zero_row
    after_home = zero_row
    for row in range(rows_y):
        home = r_lift[row, 1:2, :]
        after_out = after_out + home + jnp.where(row > my_y, r_lift[row, 0:1, :], 0.0)
        after_home = after_home + jnp.where(row < my_y, home, 0.0)
    later = later + jnp.where(row8 < HEADS, after_out, after_home)
    fin = jnp.where(
        lane8 < block,
        turned * ing * (1.0 - ing),
        pltpu.roll(tail + later, block, axis=1),
    )
    s_fin[...] = fin
    r_fin[my_x] = fin
    fin_in = x_send(9, lambda step: s_fin, r_fin.at[my_x])

    for leg in (1, 0):
        arrive(grad_q_in[leg])
        for head in range(HEADS):
            gq_ref[0, leg, :, head * dk : (head + 1) * dk] = r_q[head, leg].astype(BF16)
    for leg in (1, 0):
        arrive(out_in[leg])
        for head in range(HEADS):
            gk_ref[0, leg, :, head * dk : (head + 1) * dk] = r_out[head, leg, :, :dk].astype(BF16)
            gv_ref[0, leg, :, head * dv : (head + 1) * dv] = r_out[head, leg, :, dk:].astype(BF16)
    arrive(fin_in)
    for leg in range(2):
        rows = jnp.concatenate(
            [r_fin[head, pl.ds(leg * HEADS + my_x, 1), :] for head in range(HEADS)], axis=0
        )
        slope = 1.0 / (1.0 + jnp.exp(f_ref[0, leg].astype(F32)))
        gi_ref[0, leg] = rows[:, :block]
        gf_ref[0, leg] = rows[:, block:] * slope

    @pl.when(is_gate)
    def _():
        for step in range(1, count_dp):
            gain2(step).wait_recv()
        gain_sum = r_g2[0]
        for row in range(1, count_dp):
            gain_sum = gain_sum + r_g2[row]
        s_g3[...] = gain_sum
        r_g3[my_x] = gain_sum
        for step in range(1, HEADS * rows_y):
            gain3(step).start()

    for copy in started:
        copy.wait_send()
    for head in range(HEADS):

        @pl.when(me != head * HEADS + head)
        def _():
            where = {"ctx": head * HEADS + head}
            remote(s_g3, r_g3.at[head], g3_ss.at[0], g3_rs.at[head], where).wait_recv()

        gg_ref[2 * head : 2 * head + 2, :] = r_g3[head]

    @pl.when(is_gate)
    def _():
        for step in range(1, count_dp):
            gain2(step).wait_send()
        for step in range(1, HEADS * rows_y):
            gain3(step).wait_send()

    @pl.when(jnp.logical_not(is_gate))
    def _():
        gain1().wait_send()


def store(*refs):
    sems = refs[12]
    copies = [pltpu.make_async_copy(refs[n], refs[6 + n], sems.at[n]) for n in range(6)]
    for copy in copies:
        copy.start()
    for copy in copies:
        copy.wait()


def shards(rows_y, count_dp, queries, keys, values, out_grad, forget, inputs, gain):
    block = queries.shape[2]
    dk = queries.shape[3] // HEADS
    dv = values.shape[3] // HEADS
    part = dk // rows_y
    vmem = pltpu.VMEM
    scratch = [
        vmem(queries.shape, BF16),
        vmem(keys.shape, BF16),
        vmem(values.shape, BF16),
        vmem(out_grad.shape, BF16),
        vmem(forget.shape, BF16),
        vmem(inputs.shape, BF16),
        vmem((8, 128), BF16),
        pltpu.SemaphoreType.DMA((7,)),
        vmem((HEADS, 2, block, dk + dv), F32),
        vmem((HEADS, 2, block, dk + dv), F32),
        vmem((HEADS, 2, block, dk + dv), F32),
        vmem((HEADS, 2, block, dk + dv), F32),
        vmem((8, 128), F32),
        vmem((HEADS, 8, 128), F32),
        vmem((8, 128), F32),
        vmem((rows_y, 8, 128), F32),
        vmem((128, 128), F32),
        vmem((8, 128), F32),
        vmem((8, 128), F32),
        vmem((8, 128), F32),
        vmem((2, 2, HEADS, dk, dv), F32),
        vmem((2, 2, rows_y, part, dv), F32),
        vmem((2, 2, rows_y, part, dv), F32),
        vmem((2, 2, rows_y, part, dv), F32),
        vmem((2, 2, rows_y, part, dv), F32),
        vmem((8, dk, dv), BF16),
        vmem((8, block, block), F32),
        vmem((8, block, block), F32),
        vmem((8, block, block), BF16),
        vmem((8, block, dv), F32),
        vmem((8, block, dv), BF16),
        vmem((block, 128), F32),
        vmem((block, 128), F32),
        vmem((HEADS, 2, block, dk), F32),
        vmem((HEADS, 2, block, dk), F32),
        vmem((HEADS, 2, block, dk + dv), F32),
        vmem((HEADS, 2, block, dk + dv), F32),
        vmem((8, 128), F32),
        vmem((rows_y, 8, 128), F32),
        vmem((8, 128), F32),
        vmem((HEADS, 8, 128), F32),
        vmem((2, 128), F32),
        vmem((rows_y, 2, 128), F32),
        vmem((2, 128), F32),
        vmem((count_dp, 2, 128), F32),
        vmem((2, 128), F32),
        vmem((HEADS, 2, 128), F32),
        pltpu.SemaphoreType.DMA((11, HEADS - 1)),
        pltpu.SemaphoreType.DMA((11, HEADS - 1)),
        pltpu.SemaphoreType.DMA((11, rows_y - 1)),
        pltpu.SemaphoreType.DMA((11, rows_y - 1)),
        pltpu.SemaphoreType.DMA((max(count_dp - 1, 1),)),
        pltpu.SemaphoreType.DMA((max(count_dp - 1, 1),)),
        pltpu.SemaphoreType.DMA((1,)),
        pltpu.SemaphoreType.DMA((rows_y,)),
        pltpu.SemaphoreType.DMA((HEADS * rows_y - 1,)),
        pltpu.SemaphoreType.DMA((HEADS,)),
        pltpu.SemaphoreType.REGULAR,
    ]
    spec = pl.BlockSpec(memory_space=pltpu.VMEM)
    hbm = pl.BlockSpec(memory_space=pltpu.HBM)
    shapes = (
        jax.ShapeDtypeStruct(queries.shape, BF16),
        jax.ShapeDtypeStruct(keys.shape, BF16),
        jax.ShapeDtypeStruct(values.shape, BF16),
        jax.ShapeDtypeStruct(forget.shape, F32),
        jax.ShapeDtypeStruct(inputs.shape, F32),
        jax.ShapeDtypeStruct((8, 128), F32),
    )
    outs = pl.pallas_call(
        functools.partial(kernel, rows_y, count_dp),
        out_shape=shapes,
        in_specs=[hbm] * 7,
        out_specs=(spec,) * 6,
        scratch_shapes=scratch,
        compiler_params=pltpu.CompilerParams(
            collective_id=0, has_side_effects=True, vmem_limit_bytes=48 * 1024 * 1024
        ),
        name="mlstm_back",
    )(*[pltpu.with_memory_space_constraint(a, pltpu.HBM) for a in (queries, keys, values, out_grad, forget, inputs, gain.reshape(8, 128))])
    outs = pl.pallas_call(
        store,
        out_shape=shapes,
        in_specs=[spec] * 6,
        out_specs=(hbm,) * 6,
        scratch_shapes=[pltpu.SemaphoreType.DMA((6,))],
        compiler_params=pltpu.CompilerParams(vmem_limit_bytes=1048576),
        name="store",
    )(*outs)
    return outs[:5] + (outs[5].reshape(-1),)


def solution(mesh):
    return jax.shard_map(
        functools.partial(shards, mesh.shape["ctx"] // HEADS, mesh.shape["dp"]),
        mesh=mesh,
        in_specs=(
            P("dp", None, "ctx", None),
            P("dp", None, "ctx", None),
            P("dp", None, "ctx", None),
            P("dp", None, "ctx", None),
            P("dp", None, None, "ctx"),
            P("dp", None, None, "ctx"),
            P(),
        ),
        out_specs=(
            P("dp", None, "ctx", None),
            P("dp", None, "ctx", None),
            P("dp", None, "ctx", None),
            P("dp", None, None, "ctx"),
            P("dp", None, None, "ctx"),
            P(),
        ),
        check_vma=False,
    )
```

```python
import functools

import jax
import jax.numpy as jnp
from jax import lax
from jax.experimental import pallas as pl
from jax.experimental.pallas import tpu as pltpu
from jax.sharding import PartitionSpec as P

F32 = jnp.float32
BF16 = jnp.bfloat16
MESH = pl.DeviceIdType.MESH
HEADS = 4
CUM, ING, REACH, EARLY, WEIGHT = range(5)


def dot(left, right, left_dim, right_dim):
    return lax.dot_general(
        left, right, (((left_dim,), (right_dim,)), ((), ())), preferred_element_type=F32
    )


def twice(row):
    return jnp.concatenate([row, row], axis=1)


def kernel(
    rows_y,
    count_dp,
    q_hbm,
    k_hbm,
    v_hbm,
    g_hbm,
    f_hbm,
    i_hbm,
    gain_hbm,
    gq_ref,
    gk_ref,
    gv_ref,
    gf_ref,
    gi_ref,
    gg_ref,
    q_ref,
    k_ref,
    v_ref,
    g_ref,
    f_ref,
    i_ref,
    gain_ref,
    in_sem,
    s_kv,
    r_kv,
    s_qg,
    r_qg,
    s_gate,
    r_gate,
    s_fade,
    r_fade,
    cols,
    cum_rows,
    ing_rows,
    fade_blk,
    writes,
    totals,
    slices,
    s_state,
    r_state,
    state_b,
    scores_d,
    decay_i,
    mix_b,
    hidden_s,
    grad_b,
    ghh_cols,
    own_cols,
    s_q,
    r_q,
    s_out,
    r_out,
    s_lift,
    r_lift,
    s_fin,
    r_fin,
    s_g1,
    r_g1,
    s_g2,
    r_g2,
    s_g3,
    r_g3,
    x_ss,
    x_rs,
    y_ss,
    y_rs,
    d_ss,
    d_rs,
    g1_ss,
    g1_rs,
    g3_ss,
    g3_rs,
    ready,
):
    inputs = [
        pltpu.make_async_copy(src, dst, in_sem.at[number])
        for number, (src, dst) in enumerate(
            [
                (k_hbm, k_ref),
                (v_hbm, v_ref),
                (f_hbm, f_ref),
                (i_hbm, i_ref),
                (q_hbm, q_ref),
                (g_hbm, g_ref),
                (gain_hbm, gain_ref),
            ]
        )
    ]
    for copy in inputs:
        copy.start()
    me = lax.axis_index("ctx")
    my_dp = lax.axis_index("dp")
    my_x = lax.rem(me, HEADS)
    my_y = lax.div(me, HEADS)
    block = q_ref.shape[2]
    dk = q_ref.shape[3] // HEADS
    dv = v_ref.shape[3] // HEADS
    part = dk // rows_y

    def x_peer(step):
        return lax.rem(my_x + step, HEADS)

    def y_peer(step):
        return lax.rem(my_y + step, rows_y)

    def d_peer(step):
        return lax.rem(my_dp + step, count_dp)

    def to_x(step):
        return {"ctx": my_y * HEADS + x_peer(step)}

    def to_y(step):
        return {"ctx": y_peer(step) * HEADS + my_x}

    def to_d(step):
        return {"dp": d_peer(step)}

    started = []

    def send(src, dst, ss, rs, where):
        copy = pltpu.make_async_remote_copy(
            src_ref=src, dst_ref=dst, send_sem=ss, recv_sem=rs, device_id=where, device_id_type=MESH
        )
        copy.start()
        started.append(copy)
        return copy

    def x_send(kind, source, target):
        return [
            send(source(step), target, x_ss.at[kind, step - 1], x_rs.at[kind, step - 1], to_x(step))
            for step in range(1, HEADS)
        ]

    def y_send(kind, source, target):
        return [
            send(source(step), target, y_ss.at[kind, step - 1], y_rs.at[kind, step - 1], to_y(step))
            for step in range(1, rows_y)
        ]

    def arrive(copies):
        for copy in copies:
            copy.wait_recv()

    is_gate = my_x == my_y
    barrier = pltpu.get_barrier_semaphore()
    plane = HEADS - 1 + rows_y - 1

    def signal(sem, where):
        pl.semaphore_signal(sem, inc=1, device_id=where, device_id_type=MESH)

    for step in range(1, HEADS):

        @pl.when(x_peer(step) != my_y)
        def _():
            signal(barrier, to_x(step))

    for step in range(1, rows_y):

        @pl.when(y_peer(step) != my_x)
        def _():
            signal(barrier, to_y(step))

    @pl.when(is_gate)
    def _():
        for step in range(1, count_dp):
            signal(barrier, to_d(step))


    inputs[0].wait()
    inputs[1].wait()

    def widen(leg):
        for head in range(HEADS):
            s_kv[head, leg, :, :dk] = k_ref[0, leg, :, head * dk : (head + 1) * dk].astype(F32)
            s_kv[head, leg, :, dk:] = v_ref[0, leg, :, head * dv : (head + 1) * dv].astype(F32)

    def send_kv(leg):
        return x_send(1 + leg, lambda step: s_kv.at[x_peer(step), leg], r_kv.at[my_x, leg])

    widen(0)
    @pl.when(jnp.logical_not(is_gate))
    def _():
        pl.semaphore_wait(barrier, plane)

        @pl.when((my_y < HEADS) & (my_x == lax.rem(my_y + 1, HEADS)))
        def _():
            signal(ready, {"ctx": my_y * HEADS + my_y})

        @pl.when(my_y == lax.rem(my_x + 1, rows_y))
        def _():
            signal(ready, {"ctx": my_x * HEADS + my_x})

    @pl.when(is_gate)
    def _():
        pl.semaphore_wait(ready, 2)

    kv_in = [send_kv(0)]
    lane8 = lax.broadcasted_iota(jnp.int32, (8, 128), 1)
    row8 = lax.broadcasted_iota(jnp.int32, (8, 128), 0)
    inputs[2].wait()
    inputs[3].wait()
    forget = jnp.concatenate([f_ref[0, 0], f_ref[0, 1]], axis=0).astype(F32)
    ingate_l = jnp.concatenate([i_ref[0, 0], i_ref[0, 1]], axis=0).astype(F32)
    logsig = -jnp.log1p(jnp.exp(-forget))
    ing_own = 1.0 / (1.0 + jnp.exp(-ingate_l))
    packed = jnp.concatenate([logsig, ing_own], axis=1)
    cum = packed
    hop = 1
    while hop < block:
        cum = cum + jnp.where(
            (lane8 >= hop) & (lane8 < block), pltpu.roll(cum, hop, axis=1), 0.0
        )
        hop *= 2
    s_gate[...] = cum
    r_gate[my_x] = cum

    gate_in = x_send(0, lambda step: s_gate, r_gate.at[my_x])
    widen(1)
    kv_in.append(send_kv(1))
    for copy in inputs[4:]:
        copy.wait()
    for leg in range(2):
        r_kv[my_x, leg] = s_kv[my_x, leg]
        for head in range(HEADS):
            s_qg[head, leg, :, :dk] = q_ref[0, leg, :, head * dk : (head + 1) * dk].astype(F32)
            s_qg[head, leg, :, dk:] = g_ref[0, leg, :, head * dv : (head + 1) * dv].astype(F32)
        r_qg[my_x, leg] = s_qg[my_x, leg]

    arrive(gate_in)
    gates = jnp.concatenate(
        [
            r_gate[source, pl.ds(leg * HEADS + my_x, 1), :]
            for leg in range(2)
            for source in range(HEADS)
        ],
        axis=0,
    )
    total_log = gates[:, block - 1 : block]
    ingate = pltpu.roll(gates, block, axis=1)
    reach = jnp.exp(total_log - gates)
    cum_rows[...] = gates
    ing_rows[...] = ingate
    fade_blk[...] = jnp.broadcast_to(jnp.exp(total_log), (8, 128))
    stacked = jnp.concatenate(
        [gates, ingate, reach, jnp.exp(gates), ingate * reach, jnp.zeros((88, 128), F32)], axis=0
    )
    cols[...] = jnp.transpose(stacked)
    leg_sum = [
        jnp.sum(total_log[leg * HEADS : (leg + 1) * HEADS], axis=0, keepdims=True)
        for leg in range(2)
    ]
    row_fade = jnp.exp(jnp.where(row8 == 0, leg_sum[0], leg_sum[1]))
    s_fade[...] = row_fade
    r_fade[my_y] = row_fade
    fade_in = y_send(0, lambda step: s_fade, r_fade.at[my_y])

    def col(kind, index):
        at = kind * 8 + index
        return cols[0:block, at : at + 1]

    def fade_of(index):
        return twice(fade_blk[index : index + 1, :])

    def key_of(leg, source):
        return r_kv[source, leg, :, :dk].astype(BF16)

    def value_of(leg, source):
        return r_kv[source, leg, :, dk:].astype(BF16)

    def query_of(leg, source):
        return r_qg[source, leg, :, :dk].astype(BF16)

    onward = list(range(HEADS))
    order = [[onward, onward[::-1]], [onward[::-1], onward]]

    def send_total(phase, leg):
        path = order[phase][leg]
        total = writes[phase, leg, path[0]]
        for source in path[1:]:
            total = fade_of(leg * HEADS + source) * total + writes[phase, leg, source]
        totals[phase, leg] = total.reshape(rows_y, part, dv)
        slices[phase, leg, my_y] = totals[phase, leg, my_y]
        return y_send(
            3 + 4 * phase + 2 * leg,
            lambda step: totals.at[phase, leg, y_peer(step)],
            slices.at[phase, leg, my_y],
        )

    def scan_rows(phase, leg, path, state):
        for row in path:
            s_state[phase, leg, row] = state
            state = twice(r_fade[row, leg : leg + 1, :]) * state + slices[phase, leg, row]
        return state

    def return_rows(phase, leg):
        r_state[phase, leg, my_y] = s_state[phase, leg, my_y]
        return y_send(
            4 + 4 * phase + 2 * leg,
            lambda step: s_state.at[phase, leg, y_peer(step)],
            r_state.at[phase, leg, my_y],
        )

    slices_in = [[None, None], [None, None]]
    states_in = [[None, None], [None, None]]
    for leg in range(2):
        arrive(kv_in[leg])
        for source in range(HEADS):
            value = r_kv[source, leg, :, dk:]
            scaled = (value * col(WEIGHT, leg * HEADS + source)).astype(BF16)
            writes[0, leg, source] = dot(key_of(leg, source), scaled, 0, 0)
        slices_in[0][leg] = send_total(0, leg)

    qg_in = [
        x_send(3 + leg, lambda step, leg=leg: s_qg.at[x_peer(step), leg], r_qg.at[my_x, leg])
        for leg in (1, 0)
    ][::-1]

    row_id = lax.broadcasted_iota(jnp.int32, (block, block), 0)
    col_id = lax.broadcasted_iota(jnp.int32, (block, block), 1)
    causal = col_id >= row_id

    arrive(fade_in)
    upward = list(range(rows_y))
    zero_state = jnp.zeros((part, dv), F32)
    arrive(slices_in[0][0])
    through = scan_rows(0, 0, upward, zero_state)
    arrive(slices_in[0][1])
    scan_rows(0, 1, upward[::-1], through)
    states_in[0][1] = return_rows(0, 1)
    states_in[0][0] = return_rows(0, 0)

    for leg in (1, 0):
        arrive(qg_in[leg])
        for source in range(HEADS):
            index = leg * HEADS + source
            scores = dot(key_of(leg, source), query_of(leg, source), 1, 1)
            spread = cum_rows[index : index + 1, 0:block] - col(CUM, index)
            decay = jnp.where(causal, jnp.exp(jnp.where(causal, spread, 0.0)), 0.0)
            weighted = scores * decay
            mix = (weighted * col(ING, index)).astype(BF16)
            scores_d[index] = weighted
            decay_i[index] = decay * col(ING, index)
            mix_b[index] = mix
            hidden_s[index] = dot(mix, value_of(leg, source), 0, 0)

    def remote(src, dst, ss, rs, where):
        return pltpu.make_async_remote_copy(
            src_ref=src, dst_ref=dst, send_sem=ss, recv_sem=rs, device_id=where, device_id_type=MESH
        )

    def gain1():
        gate = {"ctx": my_x * HEADS + my_x}
        return remote(s_g1, r_g1.at[my_y], g1_ss.at[0], g1_rs.at[my_y], gate)

    def gain2(step):
        return remote(s_g2, r_g2.at[my_dp], d_ss.at[step - 1], d_rs.at[step - 1], to_d(step))

    def gain3(step):
        where = {"ctx": lax.rem(me + step, HEADS * rows_y)}
        return remote(s_g3, r_g3.at[my_x], g3_ss.at[step - 1], g3_rs.at[my_x], where)

    lane_b = lax.broadcasted_iota(jnp.int32, (block, 128), 1)
    gain_all = gain_ref[...].astype(F32)
    head_id = lax.broadcasted_iota(jnp.int32, gain_all.shape, 0)
    gain_row = jnp.concatenate(
        [
            jnp.sum(jnp.where(head_id == 2 * my_x + half, gain_all, 0.0), axis=0, keepdims=True)
            for half in range(2)
        ],
        axis=1,
    )
    gain_sum = jnp.zeros((8, dv), F32)
    ghh = jnp.zeros((block, 128), F32)
    for leg in (1, 0):
        arrive(states_in[0][leg])
        state = r_state[0, leg].reshape(dk, dv)
        for source in order[0][leg]:
            index = leg * HEADS + source
            query = query_of(leg, source)
            early = col(EARLY, index)
            rounded = state.astype(BF16)
            state_b[index] = rounded
            hidden = hidden_s[index] + early * dot(query, rounded, 1, 0)
            inv_rms = lax.rsqrt(jnp.mean(hidden * hidden, axis=1, keepdims=True) + 1e-05)
            normed = hidden * inv_rms
            out_grad = r_qg[source, leg, :, dk:]
            pushed = out_grad * gain_row
            center = jnp.mean(pushed * normed, axis=1, keepdims=True)
            grad_hidden = inv_rms * (pushed - normed * center)
            grad_b[index] = grad_hidden.astype(BF16)
            lifted = (grad_hidden * early).astype(BF16)
            writes[1, leg, source] = dot(query, lifted, 0, 0)
            gain_sum = gain_sum + jnp.sum(
                (out_grad * normed).reshape(block // 8, 8, dv), axis=0
            )
            ghh = jnp.where(
                lane_b == index, jnp.sum(grad_hidden * hidden, axis=1, keepdims=True), ghh
            )
            state = fade_of(index) * state + writes[0, leg, source]
        if leg == 0:
            gain_sum = jnp.sum(gain_sum, axis=0, keepdims=True)
            gain_sum = jnp.concatenate([gain_sum[:, :128], gain_sum[:, 128:]], axis=0)
            s_g1[...] = gain_sum
            r_g1[my_y] = gain_sum

            @pl.when(jnp.logical_not(is_gate))
            def _():
                gain1().start()

        slices_in[1][leg] = send_total(1, leg)
    ghh_cols[...] = ghh
    own_sum = jnp.zeros((block, 128), F32)
    grad_q_in = [None, None]
    for leg in (1, 0):
        for source in range(HEADS):
            index = leg * HEADS + source
            grad = grad_b[index]
            key = key_of(leg, source)
            pushed_mix = dot(value_of(leg, source), grad, 1, 1)
            attend = (pushed_mix * decay_i[index]).astype(BF16)
            own_sum = jnp.where(
                lane_b == index,
                jnp.sum(scores_d[index] * pushed_mix, axis=1, keepdims=True),
                own_sum,
            )
            s_q[source, leg] = dot(attend, key, 0, 0) + col(EARLY, index) * dot(
                grad, state_b[index], 1, 1
            )
            s_out[source, leg, :, :dk] = dot(attend, query_of(leg, source), 1, 0)
            s_out[source, leg, :, dk:] = dot(mix_b[index], grad, 1, 0)
        r_q[my_x, leg] = s_q[my_x, leg]
        grad_q_in[leg] = x_send(
            5 + leg, lambda step, leg=leg: s_q.at[x_peer(step), leg], r_q.at[my_x, leg]
        )
    own_cols[...] = own_sum

    arrive(slices_in[1][1])
    through = scan_rows(1, 1, upward, zero_state)
    states_in[1][1] = return_rows(1, 1)

    @pl.when(is_gate)
    def _():
        for step in range(1, rows_y):
            row = y_peer(step)
            remote(s_g1, r_g1.at[row], g1_ss.at[0], g1_rs.at[row], to_y(step)).wait_recv()
        gain_sum = r_g1[0]
        for row in range(1, rows_y):
            gain_sum = gain_sum + r_g1[row]
        s_g2[...] = gain_sum
        r_g2[my_dp] = gain_sum
        if count_dp > 1:
            pl.semaphore_wait(barrier, count_dp - 1)
        for step in range(1, count_dp):
            gain2(step).start()

    arrive(slices_in[1][0])
    scan_rows(1, 0, upward[::-1], through)
    states_in[1][0] = return_rows(1, 0)

    for leg in (1, 0):
        arrive(grad_q_in[leg])
        for head in range(HEADS):
            gq_ref[0, leg, :, head * dk : (head + 1) * dk] = r_q[head, leg].astype(BF16)
    own_sum = own_cols[...]
    out_in = [None, None]
    for leg in (1, 0):
        arrive(states_in[1][leg])
        state = r_state[1, leg].reshape(dk, dv)
        for source in order[1][leg]:
            index = leg * HEADS + source
            rounded = state.astype(BF16)
            weight = col(WEIGHT, index)
            carried = dot(value_of(leg, source), rounded, 1, 1)
            s_out[source, leg, :, :dk] = s_out[source, leg, :, :dk] + weight * carried
            s_out[source, leg, :, dk:] = s_out[source, leg, :, dk:] + weight * dot(
                key_of(leg, source), rounded, 1, 0
            )
            extra = col(REACH, index) * jnp.sum(
                r_kv[source, leg, :, :dk] * carried, axis=1, keepdims=True
            )
            own_sum = jnp.where(lane_b == index, own_sum + extra, own_sum)
            state = fade_of(index) * state + writes[1, leg, source]
        r_out[my_x, leg] = s_out[my_x, leg]
        out_in[leg] = x_send(
            7 + leg, lambda step, leg=leg: s_out.at[x_peer(step), leg], r_out.at[my_x, leg]
        )

    turned = jnp.transpose(jnp.concatenate([own_sum, ghh_cols[...]], axis=0))[0:8]
    ing = ing_rows[...]
    lift = pltpu.roll(turned, block, axis=1) - ing * turned
    tail = jnp.where(lane8 < block, lift, 0.0)
    hop = 1
    while hop < block:
        tail = tail + pltpu.roll(tail, 128 - hop, axis=1) * (lane8 < block - hop).astype(F32)
        hop *= 2
    sums = jnp.broadcast_to(tail[:, 0:1], (8, 128))
    leg_total = [
        jnp.sum(sums[leg * HEADS : (leg + 1) * HEADS], axis=0, keepdims=True) for leg in range(2)
    ]
    tile = jnp.where(row8 == 0, leg_total[0], leg_total[1])
    s_lift[...] = tile
    r_lift[my_y] = tile
    lift_in = y_send(1, lambda step: s_lift, r_lift.at[my_y])

    @pl.when(is_gate)
    def _():
        for step in range(1, count_dp):
            gain2(step).wait_recv()
        gain_sum = r_g2[0]
        for row in range(1, count_dp):
            gain_sum = gain_sum + r_g2[row]
        s_g3[...] = gain_sum
        r_g3[my_x] = gain_sum
        for step in range(1, HEADS * rows_y):
            gain3(step).start()


    later_rows = [None] * 8
    zero_row = jnp.zeros((1, 128), F32)
    run = zero_row
    for source in range(HEADS):
        later_rows[HEADS + source] = run
        run = run + sums[HEADS + source : HEADS + source + 1]
    run = zero_row
    for source in reversed(range(HEADS)):
        later_rows[source] = run
        run = run + sums[source : source + 1]
    later = jnp.concatenate(later_rows, axis=0)

    arrive(lift_in)
    after_out = zero_row
    after_home = zero_row
    for row in range(rows_y):
        home = r_lift[row, 1:2, :]
        after_out = after_out + home + jnp.where(row > my_y, r_lift[row, 0:1, :], 0.0)
        after_home = after_home + jnp.where(row < my_y, home, 0.0)
    later = later + jnp.where(row8 < HEADS, after_out, after_home)
    fin = jnp.where(
        lane8 < block,
        turned * ing * (1.0 - ing),
        pltpu.roll(tail + later, block, axis=1),
    )
    s_fin[...] = fin
    r_fin[my_x] = fin
    fin_in = x_send(9, lambda step: s_fin, r_fin.at[my_x])

    for leg in (1, 0):
        arrive(out_in[leg])
        for head in range(HEADS):
            gk_ref[0, leg, :, head * dk : (head + 1) * dk] = r_out[head, leg, :, :dk].astype(BF16)
            gv_ref[0, leg, :, head * dv : (head + 1) * dv] = r_out[head, leg, :, dk:].astype(BF16)
    arrive(fin_in)
    for leg in range(2):
        rows = jnp.concatenate(
            [r_fin[head, pl.ds(leg * HEADS + my_x, 1), :] for head in range(HEADS)], axis=0
        )
        slope = 1.0 / (1.0 + jnp.exp(f_ref[0, leg].astype(F32)))
        gi_ref[0, leg] = rows[:, :block]
        gf_ref[0, leg] = rows[:, block:] * slope

    for copy in started:
        copy.wait_send()
    for head in range(HEADS):

        @pl.when(me != head * HEADS + head)
        def _():
            where = {"ctx": head * HEADS + head}
            remote(s_g3, r_g3.at[head], g3_ss.at[0], g3_rs.at[head], where).wait_recv()

        gg_ref[2 * head : 2 * head + 2, :] = r_g3[head]

    @pl.when(is_gate)
    def _():
        for step in range(1, count_dp):
            gain2(step).wait_send()
        for step in range(1, HEADS * rows_y):
            gain3(step).wait_send()

    @pl.when(jnp.logical_not(is_gate))
    def _():
        gain1().wait_send()


def store(*refs):
    sems = refs[12]
    copies = [pltpu.make_async_copy(refs[n], refs[6 + n], sems.at[n]) for n in range(6)]
    for copy in copies:
        copy.start()
    for copy in copies:
        copy.wait()


def shards(rows_y, count_dp, queries, keys, values, out_grad, forget, inputs, gain):
    block = queries.shape[2]
    dk = queries.shape[3] // HEADS
    dv = values.shape[3] // HEADS
    part = dk // rows_y
    vmem = pltpu.VMEM
    scratch = [
        vmem(queries.shape, BF16),
        vmem(keys.shape, BF16),
        vmem(values.shape, BF16),
        vmem(out_grad.shape, BF16),
        vmem(forget.shape, BF16),
        vmem(inputs.shape, BF16),
        vmem((8, 128), BF16),
        pltpu.SemaphoreType.DMA((7,)),
        vmem((HEADS, 2, block, dk + dv), F32),
        vmem((HEADS, 2, block, dk + dv), F32),
        vmem((HEADS, 2, block, dk + dv), F32),
        vmem((HEADS, 2, block, dk + dv), F32),
        vmem((8, 128), F32),
        vmem((HEADS, 8, 128), F32),
        vmem((8, 128), F32),
        vmem((rows_y, 8, 128), F32),
        vmem((128, 128), F32),
        vmem((8, 128), F32),
        vmem((8, 128), F32),
        vmem((8, 128), F32),
        vmem((2, 2, HEADS, dk, dv), F32),
        vmem((2, 2, rows_y, part, dv), F32),
        vmem((2, 2, rows_y, part, dv), F32),
        vmem((2, 2, rows_y, part, dv), F32),
        vmem((2, 2, rows_y, part, dv), F32),
        vmem((8, dk, dv), BF16),
        vmem((8, block, block), F32),
        vmem((8, block, block), F32),
        vmem((8, block, block), BF16),
        vmem((8, block, dv), F32),
        vmem((8, block, dv), BF16),
        vmem((block, 128), F32),
        vmem((block, 128), F32),
        vmem((HEADS, 2, block, dk), F32),
        vmem((HEADS, 2, block, dk), F32),
        vmem((HEADS, 2, block, dk + dv), F32),
        vmem((HEADS, 2, block, dk + dv), F32),
        vmem((8, 128), F32),
        vmem((rows_y, 8, 128), F32),
        vmem((8, 128), F32),
        vmem((HEADS, 8, 128), F32),
        vmem((2, 128), F32),
        vmem((rows_y, 2, 128), F32),
        vmem((2, 128), F32),
        vmem((count_dp, 2, 128), F32),
        vmem((2, 128), F32),
        vmem((HEADS, 2, 128), F32),
        pltpu.SemaphoreType.DMA((11, HEADS - 1)),
        pltpu.SemaphoreType.DMA((11, HEADS - 1)),
        pltpu.SemaphoreType.DMA((11, rows_y - 1)),
        pltpu.SemaphoreType.DMA((11, rows_y - 1)),
        pltpu.SemaphoreType.DMA((max(count_dp - 1, 1),)),
        pltpu.SemaphoreType.DMA((max(count_dp - 1, 1),)),
        pltpu.SemaphoreType.DMA((1,)),
        pltpu.SemaphoreType.DMA((rows_y,)),
        pltpu.SemaphoreType.DMA((HEADS * rows_y - 1,)),
        pltpu.SemaphoreType.DMA((HEADS,)),
        pltpu.SemaphoreType.REGULAR,
    ]
    spec = pl.BlockSpec(memory_space=pltpu.VMEM)
    hbm = pl.BlockSpec(memory_space=pltpu.HBM)
    shapes = (
        jax.ShapeDtypeStruct(queries.shape, BF16),
        jax.ShapeDtypeStruct(keys.shape, BF16),
        jax.ShapeDtypeStruct(values.shape, BF16),
        jax.ShapeDtypeStruct(forget.shape, F32),
        jax.ShapeDtypeStruct(inputs.shape, F32),
        jax.ShapeDtypeStruct((8, 128), F32),
    )
    outs = pl.pallas_call(
        functools.partial(kernel, rows_y, count_dp),
        out_shape=shapes,
        in_specs=[hbm] * 7,
        out_specs=(spec,) * 6,
        scratch_shapes=scratch,
        compiler_params=pltpu.CompilerParams(
            collective_id=0, has_side_effects=True, vmem_limit_bytes=48 * 1024 * 1024
        ),
        name="mlstm_back",
    )(*[pltpu.with_memory_space_constraint(a, pltpu.HBM) for a in (queries, keys, values, out_grad, forget, inputs, gain.reshape(8, 128))])
    outs = pl.pallas_call(
        store,
        out_shape=shapes,
        in_specs=[spec] * 6,
        out_specs=(hbm,) * 6,
        scratch_shapes=[pltpu.SemaphoreType.DMA((6,))],
        compiler_params=pltpu.CompilerParams(vmem_limit_bytes=1048576),
        name="store",
    )(*outs)
    return outs[:5] + (outs[5].reshape(-1),)


def solution(mesh):
    return jax.shard_map(
        functools.partial(shards, mesh.shape["ctx"] // HEADS, mesh.shape["dp"]),
        mesh=mesh,
        in_specs=(
            P("dp", None, "ctx", None),
            P("dp", None, "ctx", None),
            P("dp", None, "ctx", None),
            P("dp", None, "ctx", None),
            P("dp", None, None, "ctx"),
            P("dp", None, None, "ctx"),
            P(),
        ),
        out_specs=(
            P("dp", None, "ctx", None),
            P("dp", None, "ctx", None),
            P("dp", None, "ctx", None),
            P("dp", None, None, "ctx"),
            P("dp", None, None, "ctx"),
            P(),
        ),
        check_vma=False,
    )
```

```python
import functools

import jax
import jax.numpy as jnp
from jax import lax
from jax.experimental import pallas as pl
from jax.experimental.pallas import tpu as pltpu
from jax.sharding import PartitionSpec as P

F32 = jnp.float32
BF16 = jnp.bfloat16
MESH = pl.DeviceIdType.MESH
HEADS = 4
CUM, ING, REACH, EARLY, WEIGHT = range(5)


def dot(left, right, left_dim, right_dim):
    return lax.dot_general(
        left, right, (((left_dim,), (right_dim,)), ((), ())), preferred_element_type=F32
    )


def far_first(count):
    return sorted(range(1, count), key=lambda step: -min(step, count - step))


def twice(row):
    return jnp.concatenate([row, row], axis=1)


def kernel(
    rows_y,
    count_dp,
    q_hbm,
    k_hbm,
    v_hbm,
    g_hbm,
    f_hbm,
    i_hbm,
    gain_hbm,
    gq_ref,
    gk_ref,
    gv_ref,
    gf_ref,
    gi_ref,
    gg_ref,
    q_ref,
    k_ref,
    v_ref,
    g_ref,
    f_ref,
    i_ref,
    gain_ref,
    in_sem,
    s_kv,
    r_kv,
    s_qg,
    r_qg,
    s_gate,
    r_gate,
    s_fade,
    r_fade,
    cols,
    cum_rows,
    ing_rows,
    fade_blk,
    writes,
    totals,
    slices,
    s_state,
    r_state,
    state_b,
    scores_d,
    decay_i,
    mix_b,
    hidden_s,
    grad_b,
    ghh_cols,
    own_cols,
    s_q,
    r_q,
    s_out,
    r_out,
    s_lift,
    r_lift,
    s_fin,
    r_fin,
    s_g1,
    r_g1,
    s_g2,
    r_g2,
    s_g3,
    r_g3,
    x_ss,
    x_rs,
    y_ss,
    y_rs,
    d_ss,
    d_rs,
    g1_ss,
    g1_rs,
    g3_ss,
    g3_rs,
    ready,
):
    inputs = [
        pltpu.make_async_copy(src, dst, in_sem.at[number])
        for number, (src, dst) in enumerate(
            [
                (k_hbm, k_ref),
                (v_hbm, v_ref),
                (f_hbm, f_ref),
                (i_hbm, i_ref),
                (q_hbm, q_ref),
                (g_hbm, g_ref),
                (gain_hbm, gain_ref),
            ]
        )
    ]
    for copy in inputs:
        copy.start()
    me = lax.axis_index("ctx")
    my_dp = lax.axis_index("dp")
    my_x = lax.rem(me, HEADS)
    my_y = lax.div(me, HEADS)
    block = q_ref.shape[2]
    dk = q_ref.shape[3] // HEADS
    dv = v_ref.shape[3] // HEADS
    part = dk // rows_y

    def x_peer(step):
        return lax.rem(my_x + step, HEADS)

    def y_peer(step):
        return lax.rem(my_y + step, rows_y)

    def d_peer(step):
        return lax.rem(my_dp + step, count_dp)

    def to_x(step):
        return {"ctx": my_y * HEADS + x_peer(step)}

    def to_y(step):
        return {"ctx": y_peer(step) * HEADS + my_x}

    def to_d(step):
        return {"dp": d_peer(step)}

    started = []

    def send(src, dst, ss, rs, where):
        copy = pltpu.make_async_remote_copy(
            src_ref=src, dst_ref=dst, send_sem=ss, recv_sem=rs, device_id=where, device_id_type=MESH
        )
        copy.start()
        started.append(copy)
        return copy

    def x_send(kind, source, target):
        return [
            send(source(step), target, x_ss.at[kind, step - 1], x_rs.at[kind, step - 1], to_x(step))
            for step in range(1, HEADS)
        ]

    def y_send(kind, source, target):
        return [
            send(source(step), target, y_ss.at[kind, step - 1], y_rs.at[kind, step - 1], to_y(step))
            for step in far_first(rows_y)
        ]

    def arrive(copies):
        for copy in copies:
            copy.wait_recv()

    is_gate = my_x == my_y
    barrier = pltpu.get_barrier_semaphore()
    plane = HEADS - 1 + rows_y - 1

    def signal(sem, where):
        pl.semaphore_signal(sem, inc=1, device_id=where, device_id_type=MESH)

    for step in range(1, HEADS):

        @pl.when(x_peer(step) != my_y)
        def _():
            signal(barrier, to_x(step))

    for step in range(1, rows_y):

        @pl.when(y_peer(step) != my_x)
        def _():
            signal(barrier, to_y(step))

    @pl.when(is_gate)
    def _():
        for step in range(1, count_dp):
            signal(barrier, to_d(step))


    inputs[0].wait()
    inputs[1].wait()

    def widen(leg):
        for head in range(HEADS):
            s_kv[head, leg, :, :dk] = k_ref[0, leg, :, head * dk : (head + 1) * dk].astype(F32)
            s_kv[head, leg, :, dk:] = v_ref[0, leg, :, head * dv : (head + 1) * dv].astype(F32)

    def send_kv(leg):
        return x_send(1 + leg, lambda step: s_kv.at[x_peer(step), leg], r_kv.at[my_x, leg])

    widen(0)
    @pl.when(jnp.logical_not(is_gate))
    def _():
        pl.semaphore_wait(barrier, plane)

        @pl.when((my_y < HEADS) & (my_x == lax.rem(my_y + 1, HEADS)))
        def _():
            signal(ready, {"ctx": my_y * HEADS + my_y})

        @pl.when(my_y == lax.rem(my_x + 1, rows_y))
        def _():
            signal(ready, {"ctx": my_x * HEADS + my_x})

    @pl.when(is_gate)
    def _():
        pl.semaphore_wait(ready, 2)

    kv_in = [send_kv(0)]
    lane8 = lax.broadcasted_iota(jnp.int32, (8, 128), 1)
    row8 = lax.broadcasted_iota(jnp.int32, (8, 128), 0)
    inputs[2].wait()
    inputs[3].wait()
    forget = jnp.concatenate([f_ref[0, 0], f_ref[0, 1]], axis=0).astype(F32)
    ingate_l = jnp.concatenate([i_ref[0, 0], i_ref[0, 1]], axis=0).astype(F32)
    logsig = -jnp.log1p(jnp.exp(-forget))
    ing_own = 1.0 / (1.0 + jnp.exp(-ingate_l))
    packed = jnp.concatenate([logsig, ing_own], axis=1)
    cum = packed
    hop = 1
    while hop < block:
        cum = cum + jnp.where(
            (lane8 >= hop) & (lane8 < block), pltpu.roll(cum, hop, axis=1), 0.0
        )
        hop *= 2
    s_gate[...] = cum
    r_gate[my_x] = cum

    gate_in = x_send(0, lambda step: s_gate, r_gate.at[my_x])
    widen(1)
    kv_in.append(send_kv(1))
    for copy in inputs[4:]:
        copy.wait()
    for leg in range(2):
        r_kv[my_x, leg] = s_kv[my_x, leg]
        for head in range(HEADS):
            s_qg[head, leg, :, :dk] = q_ref[0, leg, :, head * dk : (head + 1) * dk].astype(F32)
            s_qg[head, leg, :, dk:] = g_ref[0, leg, :, head * dv : (head + 1) * dv].astype(F32)
        r_qg[my_x, leg] = s_qg[my_x, leg]

    arrive(gate_in)
    gates = jnp.concatenate(
        [
            r_gate[source, pl.ds(leg * HEADS + my_x, 1), :]
            for leg in range(2)
            for source in range(HEADS)
        ],
        axis=0,
    )
    total_log = gates[:, block - 1 : block]
    ingate = pltpu.roll(gates, block, axis=1)
    reach = jnp.exp(total_log - gates)
    cum_rows[...] = gates
    ing_rows[...] = ingate
    fade_blk[...] = jnp.broadcast_to(jnp.exp(total_log), (8, 128))
    stacked = jnp.concatenate(
        [gates, ingate, reach, jnp.exp(gates), ingate * reach, jnp.zeros((88, 128), F32)], axis=0
    )
    cols[...] = jnp.transpose(stacked)
    leg_sum = [
        jnp.sum(total_log[leg * HEADS : (leg + 1) * HEADS], axis=0, keepdims=True)
        for leg in range(2)
    ]
    row_fade = jnp.exp(jnp.where(row8 == 0, leg_sum[0], leg_sum[1]))
    s_fade[...] = row_fade
    r_fade[my_y] = row_fade
    fade_in = y_send(0, lambda step: s_fade, r_fade.at[my_y])

    def col(kind, index):
        at = kind * 8 + index
        return cols[0:block, at : at + 1]

    def fade_of(index):
        return twice(fade_blk[index : index + 1, :])

    def key_of(leg, source):
        return r_kv[source, leg, :, :dk].astype(BF16)

    def value_of(leg, source):
        return r_kv[source, leg, :, dk:].astype(BF16)

    def query_of(leg, source):
        return r_qg[source, leg, :, :dk].astype(BF16)

    onward = list(range(HEADS))
    order = [[onward, onward[::-1]], [onward[::-1], onward]]

    def send_total(phase, leg):
        path = order[phase][leg]
        total = writes[phase, leg, path[0]]
        for source in path[1:]:
            total = fade_of(leg * HEADS + source) * total + writes[phase, leg, source]
        totals[phase, leg] = total.reshape(rows_y, part, dv)
        slices[phase, leg, my_y] = totals[phase, leg, my_y]
        return y_send(
            3 + 4 * phase + 2 * leg,
            lambda step: totals.at[phase, leg, y_peer(step)],
            slices.at[phase, leg, my_y],
        )

    def scan_rows(phase, leg, path, state):
        for row in path:
            s_state[phase, leg, row] = state
            state = twice(r_fade[row, leg : leg + 1, :]) * state + slices[phase, leg, row]
        return state

    def return_rows(phase, leg):
        r_state[phase, leg, my_y] = s_state[phase, leg, my_y]
        return y_send(
            4 + 4 * phase + 2 * leg,
            lambda step: s_state.at[phase, leg, y_peer(step)],
            r_state.at[phase, leg, my_y],
        )

    slices_in = [[None, None], [None, None]]
    states_in = [[None, None], [None, None]]
    for leg in range(2):
        arrive(kv_in[leg])
        for source in range(HEADS):
            value = r_kv[source, leg, :, dk:]
            scaled = (value * col(WEIGHT, leg * HEADS + source)).astype(BF16)
            writes[0, leg, source] = dot(key_of(leg, source), scaled, 0, 0)
        slices_in[0][leg] = send_total(0, leg)

    qg_in = [
        x_send(3 + leg, lambda step, leg=leg: s_qg.at[x_peer(step), leg], r_qg.at[my_x, leg])
        for leg in (1, 0)
    ][::-1]

    row_id = lax.broadcasted_iota(jnp.int32, (block, block), 0)
    col_id = lax.broadcasted_iota(jnp.int32, (block, block), 1)
    causal = col_id >= row_id

    arrive(fade_in)
    upward = list(range(rows_y))
    zero_state = jnp.zeros((part, dv), F32)
    arrive(slices_in[0][0])
    through = scan_rows(0, 0, upward, zero_state)
    arrive(slices_in[0][1])
    scan_rows(0, 1, upward[::-1], through)
    states_in[0][1] = return_rows(0, 1)
    states_in[0][0] = return_rows(0, 0)

    for leg in (1, 0):
        arrive(qg_in[leg])
        for source in range(HEADS):
            index = leg * HEADS + source
            scores = dot(key_of(leg, source), query_of(leg, source), 1, 1)
            spread = cum_rows[index : index + 1, 0:block] - col(CUM, index)
            decay = jnp.where(causal, jnp.exp(jnp.where(causal, spread, 0.0)), 0.0)
            weighted = scores * decay
            mix = (weighted * col(ING, index)).astype(BF16)
            scores_d[index] = weighted
            decay_i[index] = decay * col(ING, index)
            mix_b[index] = mix
            hidden_s[index] = dot(mix, value_of(leg, source), 0, 0)

    def remote(src, dst, ss, rs, where):
        return pltpu.make_async_remote_copy(
            src_ref=src, dst_ref=dst, send_sem=ss, recv_sem=rs, device_id=where, device_id_type=MESH
        )

    def gain1():
        gate = {"ctx": my_x * HEADS + my_x}
        return remote(s_g1, r_g1.at[my_y], g1_ss.at[0], g1_rs.at[my_y], gate)

    def gain2(step):
        return remote(s_g2, r_g2.at[my_dp], d_ss.at[step - 1], d_rs.at[step - 1], to_d(step))

    def gain3(step):
        where = {"ctx": lax.rem(me + step, HEADS * rows_y)}
        return remote(s_g3, r_g3.at[my_x], g3_ss.at[step - 1], g3_rs.at[my_x], where)

    lane_b = lax.broadcasted_iota(jnp.int32, (block, 128), 1)
    gain_all = gain_ref[...].astype(F32)
    head_id = lax.broadcasted_iota(jnp.int32, gain_all.shape, 0)
    gain_row = jnp.concatenate(
        [
            jnp.sum(jnp.where(head_id == 2 * my_x + half, gain_all, 0.0), axis=0, keepdims=True)
            for half in range(2)
        ],
        axis=1,
    )
    gain_sum = jnp.zeros((8, dv), F32)
    ghh = jnp.zeros((block, 128), F32)
    for leg in (1, 0):
        arrive(states_in[0][leg])
        state = r_state[0, leg].reshape(dk, dv)
        for source in order[0][leg]:
            index = leg * HEADS + source
            query = query_of(leg, source)
            early = col(EARLY, index)
            rounded = state.astype(BF16)
            state_b[index] = rounded
            hidden = hidden_s[index] + early * dot(query, rounded, 1, 0)
            inv_rms = lax.rsqrt(jnp.mean(hidden * hidden, axis=1, keepdims=True) + 1e-05)
            normed = hidden * inv_rms
            out_grad = r_qg[source, leg, :, dk:]
            pushed = out_grad * gain_row
            center = jnp.mean(pushed * normed, axis=1, keepdims=True)
            grad_hidden = inv_rms * (pushed - normed * center)
            grad_b[index] = grad_hidden.astype(BF16)
            lifted = (grad_hidden * early).astype(BF16)
            writes[1, leg, source] = dot(query, lifted, 0, 0)
            gain_sum = gain_sum + jnp.sum(
                (out_grad * normed).reshape(block // 8, 8, dv), axis=0
            )
            ghh = jnp.where(
                lane_b == index, jnp.sum(grad_hidden * hidden, axis=1, keepdims=True), ghh
            )
            state = fade_of(index) * state + writes[0, leg, source]
        if leg == 0:
            gain_sum = jnp.sum(gain_sum, axis=0, keepdims=True)
            gain_sum = jnp.concatenate([gain_sum[:, :128], gain_sum[:, 128:]], axis=0)
            s_g1[...] = gain_sum
            r_g1[my_y] = gain_sum

            @pl.when(jnp.logical_not(is_gate))
            def _():
                gain1().start()

        slices_in[1][leg] = send_total(1, leg)
    ghh_cols[...] = ghh
    own_sum = jnp.zeros((block, 128), F32)
    grad_q_in = [None, None]
    for leg in (1, 0):
        for source in range(HEADS):
            index = leg * HEADS + source
            grad = grad_b[index]
            key = key_of(leg, source)
            pushed_mix = dot(value_of(leg, source), grad, 1, 1)
            attend = (pushed_mix * decay_i[index]).astype(BF16)
            own_sum = jnp.where(
                lane_b == index,
                jnp.sum(scores_d[index] * pushed_mix, axis=1, keepdims=True),
                own_sum,
            )
            s_q[source, leg] = dot(attend, key, 0, 0) + col(EARLY, index) * dot(
                grad, state_b[index], 1, 1
            )
            s_out[source, leg, :, :dk] = dot(attend, query_of(leg, source), 1, 0)
            s_out[source, leg, :, dk:] = dot(mix_b[index], grad, 1, 0)
        r_q[my_x, leg] = s_q[my_x, leg]
        grad_q_in[leg] = x_send(
            5 + leg, lambda step, leg=leg: s_q.at[x_peer(step), leg], r_q.at[my_x, leg]
        )
    own_cols[...] = own_sum

    arrive(slices_in[1][1])
    through = scan_rows(1, 1, upward, zero_state)
    states_in[1][1] = return_rows(1, 1)

    @pl.when(is_gate)
    def _():
        for step in range(1, rows_y):
            row = y_peer(step)
            remote(s_g1, r_g1.at[row], g1_ss.at[0], g1_rs.at[row], to_y(step)).wait_recv()
        gain_sum = r_g1[0]
        for row in range(1, rows_y):
            gain_sum = gain_sum + r_g1[row]
        s_g2[...] = gain_sum
        r_g2[my_dp] = gain_sum
        if count_dp > 1:
            pl.semaphore_wait(barrier, count_dp - 1)
        for step in range(1, count_dp):
            gain2(step).start()

    arrive(slices_in[1][0])
    scan_rows(1, 0, upward[::-1], through)
    states_in[1][0] = return_rows(1, 0)

    for leg in (1, 0):
        arrive(grad_q_in[leg])
        for head in range(HEADS):
            gq_ref[0, leg, :, head * dk : (head + 1) * dk] = r_q[head, leg].astype(BF16)
    own_sum = own_cols[...]
    out_in = [None, None]
    for leg in (1, 0):
        arrive(states_in[1][leg])
        state = r_state[1, leg].reshape(dk, dv)
        for source in order[1][leg]:
            index = leg * HEADS + source
            rounded = state.astype(BF16)
            weight = col(WEIGHT, index)
            carried = dot(value_of(leg, source), rounded, 1, 1)
            s_out[source, leg, :, :dk] = s_out[source, leg, :, :dk] + weight * carried
            s_out[source, leg, :, dk:] = s_out[source, leg, :, dk:] + weight * dot(
                key_of(leg, source), rounded, 1, 0
            )
            extra = col(REACH, index) * jnp.sum(
                r_kv[source, leg, :, :dk] * carried, axis=1, keepdims=True
            )
            own_sum = jnp.where(lane_b == index, own_sum + extra, own_sum)
            state = fade_of(index) * state + writes[1, leg, source]
        r_out[my_x, leg] = s_out[my_x, leg]
        out_in[leg] = x_send(
            7 + leg, lambda step, leg=leg: s_out.at[x_peer(step), leg], r_out.at[my_x, leg]
        )

    turned = jnp.transpose(jnp.concatenate([own_sum, ghh_cols[...]], axis=0))[0:8]
    ing = ing_rows[...]
    lift = pltpu.roll(turned, block, axis=1) - ing * turned
    tail = jnp.where(lane8 < block, lift, 0.0)
    hop = 1
    while hop < block:
        tail = tail + pltpu.roll(tail, 128 - hop, axis=1) * (lane8 < block - hop).astype(F32)
        hop *= 2
    sums = jnp.broadcast_to(tail[:, 0:1], (8, 128))
    leg_total = [
        jnp.sum(sums[leg * HEADS : (leg + 1) * HEADS], axis=0, keepdims=True) for leg in range(2)
    ]
    tile = jnp.where(row8 == 0, leg_total[0], leg_total[1])
    s_lift[...] = tile
    r_lift[my_y] = tile
    lift_in = y_send(1, lambda step: s_lift, r_lift.at[my_y])

    @pl.when(is_gate)
    def _():
        for step in range(1, count_dp):
            gain2(step).wait_recv()
        gain_sum = r_g2[0]
        for row in range(1, count_dp):
            gain_sum = gain_sum + r_g2[row]
        s_g3[...] = gain_sum
        r_g3[my_x] = gain_sum
        for step in range(1, HEADS * rows_y):
            gain3(step).start()


    later_rows = [None] * 8
    zero_row = jnp.zeros((1, 128), F32)
    run = zero_row
    for source in range(HEADS):
        later_rows[HEADS + source] = run
        run = run + sums[HEADS + source : HEADS + source + 1]
    run = zero_row
    for source in reversed(range(HEADS)):
        later_rows[source] = run
        run = run + sums[source : source + 1]
    later = jnp.concatenate(later_rows, axis=0)

    arrive(lift_in)
    after_out = zero_row
    after_home = zero_row
    for row in range(rows_y):
        home = r_lift[row, 1:2, :]
        after_out = after_out + home + jnp.where(row > my_y, r_lift[row, 0:1, :], 0.0)
        after_home = after_home + jnp.where(row < my_y, home, 0.0)
    later = later + jnp.where(row8 < HEADS, after_out, after_home)
    fin = jnp.where(
        lane8 < block,
        turned * ing * (1.0 - ing),
        pltpu.roll(tail + later, block, axis=1),
    )
    s_fin[...] = fin
    r_fin[my_x] = fin
    fin_in = x_send(9, lambda step: s_fin, r_fin.at[my_x])

    for leg in (1, 0):
        arrive(out_in[leg])
        for head in range(HEADS):
            gk_ref[0, leg, :, head * dk : (head + 1) * dk] = r_out[head, leg, :, :dk].astype(BF16)
            gv_ref[0, leg, :, head * dv : (head + 1) * dv] = r_out[head, leg, :, dk:].astype(BF16)
    arrive(fin_in)
    for leg in range(2):
        rows = jnp.concatenate(
            [r_fin[head, pl.ds(leg * HEADS + my_x, 1), :] for head in range(HEADS)], axis=0
        )
        slope = 1.0 / (1.0 + jnp.exp(f_ref[0, leg].astype(F32)))
        gi_ref[0, leg] = rows[:, :block]
        gf_ref[0, leg] = rows[:, block:] * slope

    for copy in started:
        copy.wait_send()
    for head in range(HEADS):

        @pl.when(me != head * HEADS + head)
        def _():
            where = {"ctx": head * HEADS + head}
            remote(s_g3, r_g3.at[head], g3_ss.at[0], g3_rs.at[head], where).wait_recv()

        gg_ref[2 * head : 2 * head + 2, :] = r_g3[head]

    @pl.when(is_gate)
    def _():
        for step in range(1, count_dp):
            gain2(step).wait_send()
        for step in range(1, HEADS * rows_y):
            gain3(step).wait_send()

    @pl.when(jnp.logical_not(is_gate))
    def _():
        gain1().wait_send()


def store(*refs):
    sems = refs[12]
    copies = [pltpu.make_async_copy(refs[n], refs[6 + n], sems.at[n]) for n in range(6)]
    for copy in copies:
        copy.start()
    for copy in copies:
        copy.wait()


def shards(rows_y, count_dp, queries, keys, values, out_grad, forget, inputs, gain):
    block = queries.shape[2]
    dk = queries.shape[3] // HEADS
    dv = values.shape[3] // HEADS
    part = dk // rows_y
    vmem = pltpu.VMEM
    scratch = [
        vmem(queries.shape, BF16),
        vmem(keys.shape, BF16),
        vmem(values.shape, BF16),
        vmem(out_grad.shape, BF16),
        vmem(forget.shape, BF16),
        vmem(inputs.shape, BF16),
        vmem((8, 128), BF16),
        pltpu.SemaphoreType.DMA((7,)),
        vmem((HEADS, 2, block, dk + dv), F32),
        vmem((HEADS, 2, block, dk + dv), F32),
        vmem((HEADS, 2, block, dk + dv), F32),
        vmem((HEADS, 2, block, dk + dv), F32),
        vmem((8, 128), F32),
        vmem((HEADS, 8, 128), F32),
        vmem((8, 128), F32),
        vmem((rows_y, 8, 128), F32),
        vmem((128, 128), F32),
        vmem((8, 128), F32),
        vmem((8, 128), F32),
        vmem((8, 128), F32),
        vmem((2, 2, HEADS, dk, dv), F32),
        vmem((2, 2, rows_y, part, dv), F32),
        vmem((2, 2, rows_y, part, dv), F32),
        vmem((2, 2, rows_y, part, dv), F32),
        vmem((2, 2, rows_y, part, dv), F32),
        vmem((8, dk, dv), BF16),
        vmem((8, block, block), F32),
        vmem((8, block, block), F32),
        vmem((8, block, block), BF16),
        vmem((8, block, dv), F32),
        vmem((8, block, dv), BF16),
        vmem((block, 128), F32),
        vmem((block, 128), F32),
        vmem((HEADS, 2, block, dk), F32),
        vmem((HEADS, 2, block, dk), F32),
        vmem((HEADS, 2, block, dk + dv), F32),
        vmem((HEADS, 2, block, dk + dv), F32),
        vmem((8, 128), F32),
        vmem((rows_y, 8, 128), F32),
        vmem((8, 128), F32),
        vmem((HEADS, 8, 128), F32),
        vmem((2, 128), F32),
        vmem((rows_y, 2, 128), F32),
        vmem((2, 128), F32),
        vmem((count_dp, 2, 128), F32),
        vmem((2, 128), F32),
        vmem((HEADS, 2, 128), F32),
        pltpu.SemaphoreType.DMA((11, HEADS - 1)),
        pltpu.SemaphoreType.DMA((11, HEADS - 1)),
        pltpu.SemaphoreType.DMA((11, rows_y - 1)),
        pltpu.SemaphoreType.DMA((11, rows_y - 1)),
        pltpu.SemaphoreType.DMA((max(count_dp - 1, 1),)),
        pltpu.SemaphoreType.DMA((max(count_dp - 1, 1),)),
        pltpu.SemaphoreType.DMA((1,)),
        pltpu.SemaphoreType.DMA((rows_y,)),
        pltpu.SemaphoreType.DMA((HEADS * rows_y - 1,)),
        pltpu.SemaphoreType.DMA((HEADS,)),
        pltpu.SemaphoreType.REGULAR,
    ]
    spec = pl.BlockSpec(memory_space=pltpu.VMEM)
    hbm = pl.BlockSpec(memory_space=pltpu.HBM)
    shapes = (
        jax.ShapeDtypeStruct(queries.shape, BF16),
        jax.ShapeDtypeStruct(keys.shape, BF16),
        jax.ShapeDtypeStruct(values.shape, BF16),
        jax.ShapeDtypeStruct(forget.shape, F32),
        jax.ShapeDtypeStruct(inputs.shape, F32),
        jax.ShapeDtypeStruct((8, 128), F32),
    )
    outs = pl.pallas_call(
        functools.partial(kernel, rows_y, count_dp),
        out_shape=shapes,
        in_specs=[hbm] * 7,
        out_specs=(spec,) * 6,
        scratch_shapes=scratch,
        compiler_params=pltpu.CompilerParams(
            collective_id=0, has_side_effects=True, vmem_limit_bytes=48 * 1024 * 1024
        ),
        name="mlstm_back",
    )(*[pltpu.with_memory_space_constraint(a, pltpu.HBM) for a in (queries, keys, values, out_grad, forget, inputs, gain.reshape(8, 128))])
    outs = pl.pallas_call(
        store,
        out_shape=shapes,
        in_specs=[spec] * 6,
        out_specs=(hbm,) * 6,
        scratch_shapes=[pltpu.SemaphoreType.DMA((6,))],
        compiler_params=pltpu.CompilerParams(vmem_limit_bytes=1048576),
        name="store",
    )(*outs)
    return outs[:5] + (outs[5].reshape(-1),)


def solution(mesh):
    return jax.shard_map(
        functools.partial(shards, mesh.shape["ctx"] // HEADS, mesh.shape["dp"]),
        mesh=mesh,
        in_specs=(
            P("dp", None, "ctx", None),
            P("dp", None, "ctx", None),
            P("dp", None, "ctx", None),
            P("dp", None, "ctx", None),
            P("dp", None, None, "ctx"),
            P("dp", None, None, "ctx"),
            P(),
        ),
        out_specs=(
            P("dp", None, "ctx", None),
            P("dp", None, "ctx", None),
            P("dp", None, "ctx", None),
            P("dp", None, None, "ctx"),
            P("dp", None, None, "ctx"),
            P(),
        ),
        check_vma=False,
    )
```

```python
import functools

import jax
import jax.numpy as jnp
from jax import lax
from jax.experimental import pallas as pl
from jax.experimental.pallas import tpu as pltpu
from jax.sharding import PartitionSpec as P

F32 = jnp.float32
BF16 = jnp.bfloat16
MESH = pl.DeviceIdType.MESH
HEADS = 4
CUM, ING, REACH, EARLY, WEIGHT = range(5)


def dot(left, right, left_dim, right_dim):
    return lax.dot_general(
        left, right, (((left_dim,), (right_dim,)), ((), ())), preferred_element_type=F32
    )


def far_first(count):
    return sorted(range(1, count), key=lambda step: -min(step, count - step))


def twice(row):
    return jnp.concatenate([row, row], axis=1)


def kernel(
    rows_y,
    count_dp,
    q_hbm,
    k_hbm,
    v_hbm,
    g_hbm,
    f_hbm,
    i_hbm,
    gain_hbm,
    gq_ref,
    gk_ref,
    gv_ref,
    gf_ref,
    gi_ref,
    gg_ref,
    q_ref,
    k_ref,
    v_ref,
    g_ref,
    f_ref,
    i_ref,
    gain_ref,
    in_sem,
    s_kv,
    r_kv,
    s_qg,
    r_qg,
    s_gate,
    r_gate,
    s_fade,
    r_fade,
    cols,
    cum_rows,
    ing_rows,
    fade_blk,
    writes,
    totals,
    slices,
    s_state,
    r_state,
    state_b,
    scores_d,
    decay_i,
    mix_b,
    hidden_s,
    grad_b,
    ghh_cols,
    own_cols,
    s_q,
    r_q,
    s_out,
    r_out,
    s_lift,
    r_lift,
    s_fin,
    r_fin,
    s_g1,
    r_g1,
    s_g2,
    r_g2,
    s_g3,
    r_g3,
    x_ss,
    x_rs,
    y_ss,
    y_rs,
    d_ss,
    d_rs,
    g1_ss,
    g1_rs,
    g3_ss,
    g3_rs,
    ready,
):
    inputs = [
        pltpu.make_async_copy(src, dst, in_sem.at[number])
        for number, (src, dst) in enumerate(
            [
                (k_hbm.at[:, 0], k_ref.at[:, 0]),
                (v_hbm.at[:, 0], v_ref.at[:, 0]),
                (f_hbm, f_ref),
                (i_hbm, i_ref),
                (k_hbm.at[:, 1], k_ref.at[:, 1]),
                (v_hbm.at[:, 1], v_ref.at[:, 1]),
                (q_hbm, q_ref),
                (g_hbm, g_ref),
                (gain_hbm, gain_ref),
            ]
        )
    ]
    for copy in inputs:
        copy.start()
    me = lax.axis_index("ctx")
    my_dp = lax.axis_index("dp")
    my_x = lax.rem(me, HEADS)
    my_y = lax.div(me, HEADS)
    block = q_ref.shape[2]
    dk = q_ref.shape[3] // HEADS
    dv = v_ref.shape[3] // HEADS
    part = dk // rows_y

    def x_peer(step):
        return lax.rem(my_x + step, HEADS)

    def y_peer(step):
        return lax.rem(my_y + step, rows_y)

    def d_peer(step):
        return lax.rem(my_dp + step, count_dp)

    def to_x(step):
        return {"ctx": my_y * HEADS + x_peer(step)}

    def to_y(step):
        return {"ctx": y_peer(step) * HEADS + my_x}

    def to_d(step):
        return {"dp": d_peer(step)}

    started = []

    def send(src, dst, ss, rs, where):
        copy = pltpu.make_async_remote_copy(
            src_ref=src, dst_ref=dst, send_sem=ss, recv_sem=rs, device_id=where, device_id_type=MESH
        )
        copy.start()
        started.append(copy)
        return copy

    def x_send(kind, source, target):
        return [
            send(source(step), target, x_ss.at[kind, step - 1], x_rs.at[kind, step - 1], to_x(step))
            for step in range(1, HEADS)
        ]

    def y_send(kind, source, target):
        return [
            send(source(step), target, y_ss.at[kind, step - 1], y_rs.at[kind, step - 1], to_y(step))
            for step in far_first(rows_y)
        ]

    def arrive(copies):
        for copy in copies:
            copy.wait_recv()

    is_gate = my_x == my_y
    barrier = pltpu.get_barrier_semaphore()
    plane = HEADS - 1 + rows_y - 1

    def signal(sem, where):
        pl.semaphore_signal(sem, inc=1, device_id=where, device_id_type=MESH)

    for step in range(1, HEADS):

        @pl.when(x_peer(step) != my_y)
        def _():
            signal(barrier, to_x(step))

    for step in range(1, rows_y):

        @pl.when(y_peer(step) != my_x)
        def _():
            signal(barrier, to_y(step))

    @pl.when(is_gate)
    def _():
        for step in range(1, count_dp):
            signal(barrier, to_d(step))


    inputs[0].wait()
    inputs[1].wait()

    def widen(leg):
        for head in range(HEADS):
            s_kv[head, leg, :, :dk] = k_ref[0, leg, :, head * dk : (head + 1) * dk].astype(F32)
            s_kv[head, leg, :, dk:] = v_ref[0, leg, :, head * dv : (head + 1) * dv].astype(F32)

    def send_kv(leg):
        return x_send(1 + leg, lambda step: s_kv.at[x_peer(step), leg], r_kv.at[my_x, leg])

    widen(0)
    @pl.when(jnp.logical_not(is_gate))
    def _():
        pl.semaphore_wait(barrier, plane)

        @pl.when((my_y < HEADS) & (my_x == lax.rem(my_y + 1, HEADS)))
        def _():
            signal(ready, {"ctx": my_y * HEADS + my_y})

        @pl.when(my_y == lax.rem(my_x + 1, rows_y))
        def _():
            signal(ready, {"ctx": my_x * HEADS + my_x})

    @pl.when(is_gate)
    def _():
        pl.semaphore_wait(ready, 2)

    kv_in = [send_kv(0)]
    lane8 = lax.broadcasted_iota(jnp.int32, (8, 128), 1)
    row8 = lax.broadcasted_iota(jnp.int32, (8, 128), 0)
    inputs[2].wait()
    inputs[3].wait()
    forget = jnp.concatenate([f_ref[0, 0], f_ref[0, 1]], axis=0).astype(F32)
    ingate_l = jnp.concatenate([i_ref[0, 0], i_ref[0, 1]], axis=0).astype(F32)
    logsig = -jnp.log1p(jnp.exp(-forget))
    ing_own = 1.0 / (1.0 + jnp.exp(-ingate_l))
    packed = jnp.concatenate([logsig, ing_own], axis=1)
    cum = packed
    hop = 1
    while hop < block:
        cum = cum + jnp.where(
            (lane8 >= hop) & (lane8 < block), pltpu.roll(cum, hop, axis=1), 0.0
        )
        hop *= 2
    s_gate[...] = cum
    r_gate[my_x] = cum

    gate_in = x_send(0, lambda step: s_gate, r_gate.at[my_x])
    inputs[4].wait()
    inputs[5].wait()
    widen(1)
    kv_in.append(send_kv(1))
    for copy in inputs[6:]:
        copy.wait()
    for leg in range(2):
        r_kv[my_x, leg] = s_kv[my_x, leg]
        for head in range(HEADS):
            s_qg[head, leg, :, :dk] = q_ref[0, leg, :, head * dk : (head + 1) * dk].astype(F32)
            s_qg[head, leg, :, dk:] = g_ref[0, leg, :, head * dv : (head + 1) * dv].astype(F32)
        r_qg[my_x, leg] = s_qg[my_x, leg]

    arrive(gate_in)
    gates = jnp.concatenate(
        [
            r_gate[source, pl.ds(leg * HEADS + my_x, 1), :]
            for leg in range(2)
            for source in range(HEADS)
        ],
        axis=0,
    )
    total_log = gates[:, block - 1 : block]
    ingate = pltpu.roll(gates, block, axis=1)
    reach = jnp.exp(total_log - gates)
    cum_rows[...] = gates
    ing_rows[...] = ingate
    fade_blk[...] = jnp.broadcast_to(jnp.exp(total_log), (8, 128))
    stacked = jnp.concatenate(
        [gates, ingate, reach, jnp.exp(gates), ingate * reach, jnp.zeros((88, 128), F32)], axis=0
    )
    cols[...] = jnp.transpose(stacked)
    leg_sum = [
        jnp.sum(total_log[leg * HEADS : (leg + 1) * HEADS], axis=0, keepdims=True)
        for leg in range(2)
    ]
    row_fade = jnp.exp(jnp.where(row8 == 0, leg_sum[0], leg_sum[1]))
    s_fade[...] = row_fade
    r_fade[my_y] = row_fade
    fade_in = y_send(0, lambda step: s_fade, r_fade.at[my_y])

    def col(kind, index):
        at = kind * 8 + index
        return cols[0:block, at : at + 1]

    def fade_of(index):
        return twice(fade_blk[index : index + 1, :])

    def key_of(leg, source):
        return r_kv[source, leg, :, :dk].astype(BF16)

    def value_of(leg, source):
        return r_kv[source, leg, :, dk:].astype(BF16)

    def query_of(leg, source):
        return r_qg[source, leg, :, :dk].astype(BF16)

    onward = list(range(HEADS))
    order = [[onward, onward[::-1]], [onward[::-1], onward]]

    def send_total(phase, leg):
        path = order[phase][leg]
        total = writes[phase, leg, path[0]]
        for source in path[1:]:
            total = fade_of(leg * HEADS + source) * total + writes[phase, leg, source]
        totals[phase, leg] = total.reshape(rows_y, part, dv)
        slices[phase, leg, my_y] = totals[phase, leg, my_y]
        return y_send(
            3 + 4 * phase + 2 * leg,
            lambda step: totals.at[phase, leg, y_peer(step)],
            slices.at[phase, leg, my_y],
        )

    def scan_rows(phase, leg, path, state):
        for row in path:
            s_state[phase, leg, row] = state
            state = twice(r_fade[row, leg : leg + 1, :]) * state + slices[phase, leg, row]
        return state

    def return_rows(phase, leg):
        r_state[phase, leg, my_y] = s_state[phase, leg, my_y]
        return y_send(
            4 + 4 * phase + 2 * leg,
            lambda step: s_state.at[phase, leg, y_peer(step)],
            r_state.at[phase, leg, my_y],
        )

    slices_in = [[None, None], [None, None]]
    states_in = [[None, None], [None, None]]
    for leg in range(2):
        arrive(kv_in[leg])
        for source in range(HEADS):
            value = r_kv[source, leg, :, dk:]
            scaled = (value * col(WEIGHT, leg * HEADS + source)).astype(BF16)
            writes[0, leg, source] = dot(key_of(leg, source), scaled, 0, 0)
        slices_in[0][leg] = send_total(0, leg)

    qg_in = [
        x_send(3 + leg, lambda step, leg=leg: s_qg.at[x_peer(step), leg], r_qg.at[my_x, leg])
        for leg in (1, 0)
    ][::-1]

    row_id = lax.broadcasted_iota(jnp.int32, (block, block), 0)
    col_id = lax.broadcasted_iota(jnp.int32, (block, block), 1)
    causal = col_id >= row_id

    arrive(fade_in)
    upward = list(range(rows_y))
    zero_state = jnp.zeros((part, dv), F32)
    arrive(slices_in[0][0])
    through = scan_rows(0, 0, upward, zero_state)
    arrive(slices_in[0][1])
    scan_rows(0, 1, upward[::-1], through)
    states_in[0][1] = return_rows(0, 1)
    states_in[0][0] = return_rows(0, 0)

    for leg in (1, 0):
        arrive(qg_in[leg])
        for source in range(HEADS):
            index = leg * HEADS + source
            scores = dot(key_of(leg, source), query_of(leg, source), 1, 1)
            spread = cum_rows[index : index + 1, 0:block] - col(CUM, index)
            decay = jnp.where(causal, jnp.exp(jnp.where(causal, spread, 0.0)), 0.0)
            weighted = scores * decay
            mix = (weighted * col(ING, index)).astype(BF16)
            scores_d[index] = weighted
            decay_i[index] = decay * col(ING, index)
            mix_b[index] = mix
            hidden_s[index] = dot(mix, value_of(leg, source), 0, 0)

    def remote(src, dst, ss, rs, where):
        return pltpu.make_async_remote_copy(
            src_ref=src, dst_ref=dst, send_sem=ss, recv_sem=rs, device_id=where, device_id_type=MESH
        )

    def gain1():
        gate = {"ctx": my_x * HEADS + my_x}
        return remote(s_g1, r_g1.at[my_y], g1_ss.at[0], g1_rs.at[my_y], gate)

    def gain2(step):
        return remote(s_g2, r_g2.at[my_dp], d_ss.at[step - 1], d_rs.at[step - 1], to_d(step))

    def gain3(step):
        where = {"ctx": lax.rem(me + step, HEADS * rows_y)}
        return remote(s_g3, r_g3.at[my_x], g3_ss.at[step - 1], g3_rs.at[my_x], where)

    lane_b = lax.broadcasted_iota(jnp.int32, (block, 128), 1)
    gain_all = gain_ref[...].astype(F32)
    head_id = lax.broadcasted_iota(jnp.int32, gain_all.shape, 0)
    gain_row = jnp.concatenate(
        [
            jnp.sum(jnp.where(head_id == 2 * my_x + half, gain_all, 0.0), axis=0, keepdims=True)
            for half in range(2)
        ],
        axis=1,
    )
    gain_sum = jnp.zeros((8, dv), F32)
    ghh = jnp.zeros((block, 128), F32)
    for leg in (1, 0):
        arrive(states_in[0][leg])
        state = r_state[0, leg].reshape(dk, dv)
        for source in order[0][leg]:
            index = leg * HEADS + source
            query = query_of(leg, source)
            early = col(EARLY, index)
            rounded = state.astype(BF16)
            state_b[index] = rounded
            hidden = hidden_s[index] + early * dot(query, rounded, 1, 0)
            inv_rms = lax.rsqrt(jnp.mean(hidden * hidden, axis=1, keepdims=True) + 1e-05)
            normed = hidden * inv_rms
            out_grad = r_qg[source, leg, :, dk:]
            pushed = out_grad * gain_row
            center = jnp.mean(pushed * normed, axis=1, keepdims=True)
            grad_hidden = inv_rms * (pushed - normed * center)
            grad_b[index] = grad_hidden.astype(BF16)
            lifted = (grad_hidden * early).astype(BF16)
            writes[1, leg, source] = dot(query, lifted, 0, 0)
            gain_sum = gain_sum + jnp.sum(
                (out_grad * normed).reshape(block // 8, 8, dv), axis=0
            )
            ghh = jnp.where(
                lane_b == index, jnp.sum(grad_hidden * hidden, axis=1, keepdims=True), ghh
            )
            state = fade_of(index) * state + writes[0, leg, source]
        if leg == 0:
            gain_sum = jnp.sum(gain_sum, axis=0, keepdims=True)
            gain_sum = jnp.concatenate([gain_sum[:, :128], gain_sum[:, 128:]], axis=0)
            s_g1[...] = gain_sum
            r_g1[my_y] = gain_sum

            @pl.when(jnp.logical_not(is_gate))
            def _():
                gain1().start()

        slices_in[1][leg] = send_total(1, leg)
    ghh_cols[...] = ghh
    own_sum = jnp.zeros((block, 128), F32)
    grad_q_in = [None, None]
    for leg in (1, 0):
        for source in range(HEADS):
            index = leg * HEADS + source
            grad = grad_b[index]
            key = key_of(leg, source)
            pushed_mix = dot(value_of(leg, source), grad, 1, 1)
            attend = (pushed_mix * decay_i[index]).astype(BF16)
            own_sum = jnp.where(
                lane_b == index,
                jnp.sum(scores_d[index] * pushed_mix, axis=1, keepdims=True),
                own_sum,
            )
            s_q[source, leg] = dot(attend, key, 0, 0) + col(EARLY, index) * dot(
                grad, state_b[index], 1, 1
            )
            s_out[source, leg, :, :dk] = dot(attend, query_of(leg, source), 1, 0)
            s_out[source, leg, :, dk:] = dot(mix_b[index], grad, 1, 0)
        r_q[my_x, leg] = s_q[my_x, leg]
        grad_q_in[leg] = x_send(
            5 + leg, lambda step, leg=leg: s_q.at[x_peer(step), leg], r_q.at[my_x, leg]
        )
    own_cols[...] = own_sum

    arrive(slices_in[1][1])
    through = scan_rows(1, 1, upward, zero_state)
    states_in[1][1] = return_rows(1, 1)

    @pl.when(is_gate)
    def _():
        for step in range(1, rows_y):
            row = y_peer(step)
            remote(s_g1, r_g1.at[row], g1_ss.at[0], g1_rs.at[row], to_y(step)).wait_recv()
        gain_sum = r_g1[0]
        for row in range(1, rows_y):
            gain_sum = gain_sum + r_g1[row]
        s_g2[...] = gain_sum
        r_g2[my_dp] = gain_sum
        if count_dp > 1:
            pl.semaphore_wait(barrier, count_dp - 1)
        for step in far_first(count_dp):
            gain2(step).start()

    arrive(slices_in[1][0])
    scan_rows(1, 0, upward[::-1], through)
    states_in[1][0] = return_rows(1, 0)

    for leg in (1, 0):
        arrive(grad_q_in[leg])
        for head in range(HEADS):
            gq_ref[0, leg, :, head * dk : (head + 1) * dk] = r_q[head, leg].astype(BF16)
    own_sum = own_cols[...]
    out_in = [None, None]
    for leg in (1, 0):
        arrive(states_in[1][leg])
        state = r_state[1, leg].reshape(dk, dv)
        for source in order[1][leg]:
            index = leg * HEADS + source
            rounded = state.astype(BF16)
            weight = col(WEIGHT, index)
            carried = dot(value_of(leg, source), rounded, 1, 1)
            s_out[source, leg, :, :dk] = s_out[source, leg, :, :dk] + weight * carried
            s_out[source, leg, :, dk:] = s_out[source, leg, :, dk:] + weight * dot(
                key_of(leg, source), rounded, 1, 0
            )
            extra = col(REACH, index) * jnp.sum(
                r_kv[source, leg, :, :dk] * carried, axis=1, keepdims=True
            )
            own_sum = jnp.where(lane_b == index, own_sum + extra, own_sum)
            state = fade_of(index) * state + writes[1, leg, source]
        r_out[my_x, leg] = s_out[my_x, leg]
        out_in[leg] = x_send(
            7 + leg, lambda step, leg=leg: s_out.at[x_peer(step), leg], r_out.at[my_x, leg]
        )

    turned = jnp.transpose(jnp.concatenate([own_sum, ghh_cols[...]], axis=0))[0:8]
    ing = ing_rows[...]
    lift = pltpu.roll(turned, block, axis=1) - ing * turned
    tail = jnp.where(lane8 < block, lift, 0.0)
    hop = 1
    while hop < block:
        tail = tail + pltpu.roll(tail, 128 - hop, axis=1) * (lane8 < block - hop).astype(F32)
        hop *= 2
    sums = jnp.broadcast_to(tail[:, 0:1], (8, 128))
    leg_total = [
        jnp.sum(sums[leg * HEADS : (leg + 1) * HEADS], axis=0, keepdims=True) for leg in range(2)
    ]
    tile = jnp.where(row8 == 0, leg_total[0], leg_total[1])
    s_lift[...] = tile
    r_lift[my_y] = tile
    lift_in = y_send(1, lambda step: s_lift, r_lift.at[my_y])

    @pl.when(is_gate)
    def _():
        for step in range(1, count_dp):
            gain2(step).wait_recv()
        gain_sum = r_g2[0]
        for row in range(1, count_dp):
            gain_sum = gain_sum + r_g2[row]
        s_g3[...] = gain_sum
        r_g3[my_x] = gain_sum
        for step in far_first(HEADS * rows_y):
            gain3(step).start()


    later_rows = [None] * 8
    zero_row = jnp.zeros((1, 128), F32)
    run = zero_row
    for source in range(HEADS):
        later_rows[HEADS + source] = run
        run = run + sums[HEADS + source : HEADS + source + 1]
    run = zero_row
    for source in reversed(range(HEADS)):
        later_rows[source] = run
        run = run + sums[source : source + 1]
    later = jnp.concatenate(later_rows, axis=0)

    arrive(lift_in)
    after_out = zero_row
    after_home = zero_row
    for row in range(rows_y):
        home = r_lift[row, 1:2, :]
        after_out = after_out + home + jnp.where(row > my_y, r_lift[row, 0:1, :], 0.0)
        after_home = after_home + jnp.where(row < my_y, home, 0.0)
    later = later + jnp.where(row8 < HEADS, after_out, after_home)
    fin = jnp.where(
        lane8 < block,
        turned * ing * (1.0 - ing),
        pltpu.roll(tail + later, block, axis=1),
    )
    s_fin[...] = fin
    r_fin[my_x] = fin
    fin_in = x_send(9, lambda step: s_fin, r_fin.at[my_x])

    for leg in (1, 0):
        arrive(out_in[leg])
        for head in range(HEADS):
            gk_ref[0, leg, :, head * dk : (head + 1) * dk] = r_out[head, leg, :, :dk].astype(BF16)
            gv_ref[0, leg, :, head * dv : (head + 1) * dv] = r_out[head, leg, :, dk:].astype(BF16)
    arrive(fin_in)
    for leg in range(2):
        rows = jnp.concatenate(
            [r_fin[head, pl.ds(leg * HEADS + my_x, 1), :] for head in range(HEADS)], axis=0
        )
        slope = 1.0 / (1.0 + jnp.exp(f_ref[0, leg].astype(F32)))
        gi_ref[0, leg] = rows[:, :block]
        gf_ref[0, leg] = rows[:, block:] * slope

    for copy in started:
        copy.wait_send()
    for head in range(HEADS):

        @pl.when(me != head * HEADS + head)
        def _():
            where = {"ctx": head * HEADS + head}
            remote(s_g3, r_g3.at[head], g3_ss.at[0], g3_rs.at[head], where).wait_recv()

        gg_ref[2 * head : 2 * head + 2, :] = r_g3[head]

    @pl.when(is_gate)
    def _():
        for step in range(1, count_dp):
            gain2(step).wait_send()
        for step in range(1, HEADS * rows_y):
            gain3(step).wait_send()

    @pl.when(jnp.logical_not(is_gate))
    def _():
        gain1().wait_send()


def store(*refs):
    sems = refs[12]
    copies = [pltpu.make_async_copy(refs[n], refs[6 + n], sems.at[n]) for n in range(6)]
    for copy in copies:
        copy.start()
    for copy in copies:
        copy.wait()


def shards(rows_y, count_dp, queries, keys, values, out_grad, forget, inputs, gain):
    block = queries.shape[2]
    dk = queries.shape[3] // HEADS
    dv = values.shape[3] // HEADS
    part = dk // rows_y
    vmem = pltpu.VMEM
    scratch = [
        vmem(queries.shape, BF16),
        vmem(keys.shape, BF16),
        vmem(values.shape, BF16),
        vmem(out_grad.shape, BF16),
        vmem(forget.shape, BF16),
        vmem(inputs.shape, BF16),
        vmem((8, 128), BF16),
        pltpu.SemaphoreType.DMA((9,)),
        vmem((HEADS, 2, block, dk + dv), F32),
        vmem((HEADS, 2, block, dk + dv), F32),
        vmem((HEADS, 2, block, dk + dv), F32),
        vmem((HEADS, 2, block, dk + dv), F32),
        vmem((8, 128), F32),
        vmem((HEADS, 8, 128), F32),
        vmem((8, 128), F32),
        vmem((rows_y, 8, 128), F32),
        vmem((128, 128), F32),
        vmem((8, 128), F32),
        vmem((8, 128), F32),
        vmem((8, 128), F32),
        vmem((2, 2, HEADS, dk, dv), F32),
        vmem((2, 2, rows_y, part, dv), F32),
        vmem((2, 2, rows_y, part, dv), F32),
        vmem((2, 2, rows_y, part, dv), F32),
        vmem((2, 2, rows_y, part, dv), F32),
        vmem((8, dk, dv), BF16),
        vmem((8, block, block), F32),
        vmem((8, block, block), F32),
        vmem((8, block, block), BF16),
        vmem((8, block, dv), F32),
        vmem((8, block, dv), BF16),
        vmem((block, 128), F32),
        vmem((block, 128), F32),
        vmem((HEADS, 2, block, dk), F32),
        vmem((HEADS, 2, block, dk), F32),
        vmem((HEADS, 2, block, dk + dv), F32),
        vmem((HEADS, 2, block, dk + dv), F32),
        vmem((8, 128), F32),
        vmem((rows_y, 8, 128), F32),
        vmem((8, 128), F32),
        vmem((HEADS, 8, 128), F32),
        vmem((2, 128), F32),
        vmem((rows_y, 2, 128), F32),
        vmem((2, 128), F32),
        vmem((count_dp, 2, 128), F32),
        vmem((2, 128), F32),
        vmem((HEADS, 2, 128), F32),
        pltpu.SemaphoreType.DMA((11, HEADS - 1)),
        pltpu.SemaphoreType.DMA((11, HEADS - 1)),
        pltpu.SemaphoreType.DMA((11, rows_y - 1)),
        pltpu.SemaphoreType.DMA((11, rows_y - 1)),
        pltpu.SemaphoreType.DMA((max(count_dp - 1, 1),)),
        pltpu.SemaphoreType.DMA((max(count_dp - 1, 1),)),
        pltpu.SemaphoreType.DMA((1,)),
        pltpu.SemaphoreType.DMA((rows_y,)),
        pltpu.SemaphoreType.DMA((HEADS * rows_y - 1,)),
        pltpu.SemaphoreType.DMA((HEADS,)),
        pltpu.SemaphoreType.REGULAR,
    ]
    spec = pl.BlockSpec(memory_space=pltpu.VMEM)
    hbm = pl.BlockSpec(memory_space=pltpu.HBM)
    shapes = (
        jax.ShapeDtypeStruct(queries.shape, BF16),
        jax.ShapeDtypeStruct(keys.shape, BF16),
        jax.ShapeDtypeStruct(values.shape, BF16),
        jax.ShapeDtypeStruct(forget.shape, F32),
        jax.ShapeDtypeStruct(inputs.shape, F32),
        jax.ShapeDtypeStruct((8, 128), F32),
    )
    outs = pl.pallas_call(
        functools.partial(kernel, rows_y, count_dp),
        out_shape=shapes,
        in_specs=[hbm] * 7,
        out_specs=(spec,) * 6,
        scratch_shapes=scratch,
        compiler_params=pltpu.CompilerParams(
            collective_id=0, has_side_effects=True, vmem_limit_bytes=48 * 1024 * 1024
        ),
        name="mlstm_back",
    )(*[pltpu.with_memory_space_constraint(a, pltpu.HBM) for a in (queries, keys, values, out_grad, forget, inputs, gain.reshape(8, 128))])
    outs = pl.pallas_call(
        store,
        out_shape=shapes,
        in_specs=[spec] * 6,
        out_specs=(hbm,) * 6,
        scratch_shapes=[pltpu.SemaphoreType.DMA((6,))],
        compiler_params=pltpu.CompilerParams(vmem_limit_bytes=1048576),
        name="store",
    )(*outs)
    return outs[:5] + (outs[5].reshape(-1),)


def solution(mesh):
    return jax.shard_map(
        functools.partial(shards, mesh.shape["ctx"] // HEADS, mesh.shape["dp"]),
        mesh=mesh,
        in_specs=(
            P("dp", None, "ctx", None),
            P("dp", None, "ctx", None),
            P("dp", None, "ctx", None),
            P("dp", None, "ctx", None),
            P("dp", None, None, "ctx"),
            P("dp", None, None, "ctx"),
            P(),
        ),
        out_specs=(
            P("dp", None, "ctx", None),
            P("dp", None, "ctx", None),
            P("dp", None, "ctx", None),
            P("dp", None, None, "ctx"),
            P("dp", None, None, "ctx"),
            P(),
        ),
        check_vma=False,
    )
```
